256 devices in a mesh: group: 128 (over z, y, x), seq: 2 (over core).
Axes of the slice: x: 4, y: 4, z: 8, core: 2. Of those that a mesh axis runs over, the one named last changes fastest.
Arguments:
- tokens: bfloat16 [65536, 1024], P(('group', 'seq')), may hold values from -12 to 12
- w_query: bfloat16 [1024, 1024], P(None, 'seq'), may hold values from -12.5 to 12.5
- w_key: bfloat16 [1024, 1024], P(None, 'seq'), may hold values from -0.1875 to 0.1875
- w_value: bfloat16 [1024, 1024], P(None, 'seq'), may hold values from -0.1875 to 0.1875
- w_out: bfloat16 [1024, 1024], P(None, 'seq'), may hold values from -0.1875 to 0.1875
- slot_query: bfloat16 [64, 1024], P(None, 'seq'), may hold values from -1300 to 1300
- span_decay: float32 [128, 8], P('group', 'seq'), may hold values from 0 to 6.7, as said below
- ffn_up: bfloat16 [1024, 4096], P('group', 'seq'), may hold values from -0.1875 to 0.1875
- ffn_down: bfloat16 [4096, 1024], P('seq', 'group'), may hold values from -0.09375 to 0.09375
- norm_gain: float32 [1024], replicated, may hold values from 0.5 to 1.5
Outputs:
- outputs: bfloat16 [65536, 1024], P('group', 'seq')
The draws below stay inside these ranges and needn't reach their ends.
Inputs may be any that keep to these rules, and one draw needn't show every extreme that they name: `span_decay`: nonnegative per-span log decays.
All inputs are finite; a program needn't handle non-finite values.
Results may differ from the reference program's by a relative error of at most 0.02.
The reference program's roundings to bfloat16 on the way count: a program that leaves them out, or rounds other values in their place, can miss the bound.
Values may be sent and summed in bfloat16 or wider, within the bound.
A program may use at most 128 MiB of HBM per device.

```python
import math
import jax
import jax.numpy as jnp
from jax import lax

D = 1024
ATTENDER_NUMBER = 8
HS = 128
FF = 4096
MEM = 64
WIN = 512
CL = 512
STRETCH_NUMBER = 128
TOKENS = 65536


def draw_tokens(key, part):
    noise_key, direction_key, picked_key, strength_key, forced_key = jax.random.split(key, 5)
    base = jnp.clip(jax.random.normal(noise_key, (TOKENS, D), jnp.float32), -6.0, 6.0)
    directions = jnp.clip(jax.random.normal(direction_key, (STRETCH_NUMBER, D), jnp.float32), -4.0, 4.0)
    forced = jnp.arange(STRETCH_NUMBER, dtype=jnp.int32) == jax.random.randint(forced_key, (), 0, STRETCH_NUMBER)
    strong = (jax.random.uniform(picked_key, (STRETCH_NUMBER,), jnp.float32) < 0.125) | forced
    strengths = jnp.where(strong, jax.random.uniform(strength_key, (STRETCH_NUMBER,), jnp.float32, 1.2, 1.5), 0.3)
    common = strengths[:, None] * directions
    whole = base.reshape(STRETCH_NUMBER, CL, D) + common[:, None, :]
    return whole.reshape(TOKENS, D).astype(jnp.bfloat16)


def draw_w_query(key, part):
    base = jnp.clip(jax.random.normal(key, (D, D), jnp.float32), -4.0, 4.0) * (2.5 / math.sqrt(D))
    return base.astype(jnp.bfloat16)


def draw_slot_query(key, part):
    base = jnp.clip(jax.random.normal(key, (MEM, D), jnp.float32), -4.0, 4.0)
    strata = jax.random.permutation(jax.random.fold_in(key, 3), jnp.arange(MEM, dtype=jnp.int32)).astype(jnp.float32)
    offsets = jax.random.uniform(jax.random.fold_in(key, 5), (MEM,), jnp.float32, 0.0, 1.0)
    low_log = math.log(0.08)
    high_log = math.log(10.0)
    slot_scale = jnp.exp(low_log + (high_log - low_log) * (strata + offsets) / MEM)
    jitter = jnp.exp(jax.random.uniform(jax.random.fold_in(key, 6), (MEM, ATTENDER_NUMBER), jnp.float32, math.log(0.6), math.log(1.6)))
    base = base * jnp.repeat(slot_scale[:, None] * jitter, HS, axis=1)
    return base.astype(jnp.bfloat16)


def draw_span_decay(key, part):
    first, second, ternary_multiplier, quaternary_multiplier = jax.random.split(key, 4)
    lower = 0.1 / STRETCH_NUMBER
    upper = 3.0
    fading_speeds = jnp.exp(jax.random.uniform(first, (ATTENDER_NUMBER,), jnp.float32, math.log(lower), math.log(upper)))
    stochastic_perturbation = jax.random.uniform(second, (STRETCH_NUMBER, ATTENDER_NUMBER), jnp.float32, 0.5, 2.0)
    cluster_batches = jnp.where(jax.random.uniform(ternary_multiplier, (STRETCH_NUMBER, ATTENDER_NUMBER), jnp.float32) < 3.0 / STRETCH_NUMBER, jax.random.uniform(quaternary_multiplier, (STRETCH_NUMBER, ATTENDER_NUMBER), jnp.float32, 0.22, 0.7), 0.0)
    return fading_speeds[None, :] * stochastic_perturbation + cluster_batches


def shard_levels(key, extent, pieces, low, largest):
    loudness, own = 1.0, jax.random.fold_in(key, 6)
    for axis_at, blocks in pieces:
        heights = jnp.exp(jax.random.uniform(jax.random.fold_in(own, axis_at), (blocks,), jnp.float32, low / len(pieces), largest / len(pieces)))
        loudness = loudness * jnp.repeat(heights, extent[axis_at] // blocks).reshape([-1 if axis == axis_at else 1 for axis in range(len(extent))])
    return loudness


def centred(own_key, shape, width, most, pieces=(), kind=jnp.bfloat16):
    entries = jax.random.normal(own_key, shape, jnp.float32) * width
    if len(pieces) > 0:
        entries = shard_levels(own_key, shape, pieces, -0.22, 0.18) * entries
    return jnp.clip(entries, min=-most, max=most).astype(kind)


def setup_inputs(seed: int = 0) -> dict:
    key_list = jax.random.split(jax.random.key(seed), 11)
    return {
        "tokens": draw_tokens(jax.random.fold_in(key_list[10], 71), 0),
        "w_query": draw_w_query(jax.random.fold_in(key_list[10], 71), 0),
        "w_key": centred(key_list[2], (D, D), D ** -0.5, 0.1875, ((1, 2),)),
        "w_value": centred(key_list[3], (D, D), D ** -0.5, 0.1875, ((1, 2),)),
        "w_out": centred(key_list[4], (D, D), D ** -0.5, 0.1875, ((1, 2),)),
        "slot_query": draw_slot_query(jax.random.fold_in(key_list[10], 71), 0),
        "span_decay": draw_span_decay(jax.random.fold_in(key_list[10], 71), 0),
        "ffn_up": centred(key_list[7], (D, FF), D ** -0.5, 0.1875, ((0, 128), (1, 2))),
        "ffn_down": centred(key_list[8], (FF, D), FF ** -0.5, 0.09375, ((0, 2), (1, 128))),
        "norm_gain": jnp.clip(1.0 + 0.1 * jax.random.normal(key_list[9], (D,), jnp.float32), 0.5, 1.5),
    }


floor_logit = -1e+30
null_logit = 8.0

def merge_states(earlier, later_state):
    rate_a, peak_a, mass_a, value_a = earlier
    rate_b, peak_b, mass_b, value_b = later_state
    shifted = peak_a - rate_b[..., None]
    highest = jnp.maximum(shifted, peak_b)
    factor_a = jnp.exp(shifted - highest)
    factor_b = jnp.exp(peak_b - highest)
    return (rate_a + rate_b, highest, mass_a * factor_a + mass_b * factor_b, value_a * factor_a[..., None] + value_b * factor_b[..., None])

def finish_memory(state):
    rate_sum, peak_val, mass_sum, weighted = state
    anchor = jnp.maximum(peak_val, null_logit)
    factor = jnp.exp(peak_val - anchor)
    denom = mass_sum * factor + jnp.exp(null_logit - anchor)
    return weighted * (factor / denom)[..., None]

def settle(memory, ffn_total, norm_gain):
    summed = memory.astype(jnp.float32) + ffn_total
    scaled = summed * lax.rsqrt(lax.optimization_barrier(jnp.mean(summed * summed, axis=-1, keepdims=True)) + 1e-06)
    return (scaled * norm_gain).astype(jnp.bfloat16)

def rounded(values):
    return lax.optimization_barrier(values.astype(jnp.bfloat16)).astype(jnp.float32)

def window_block(block_queries, block_keys, block_values, first_valid, mem_keys, mem_values):
    scale = HS ** (-0.5)
    queries_f = block_queries.astype(jnp.float32)
    scores = jnp.einsum('qhd,khd->hqk', queries_f, block_keys.astype(jnp.float32)) * scale
    row_pos = jnp.arange(WIN, dtype=jnp.int32)[:, None]
    col_pos = jnp.arange(2 * WIN, dtype=jnp.int32)[None, :]
    allowed = (col_pos > row_pos) & (col_pos <= row_pos + WIN) & (col_pos >= first_valid)
    scores = jnp.where(allowed[None], scores, floor_logit)
    probs = jnp.exp(scores - lax.optimization_barrier(jnp.max(scores, axis=-1, keepdims=True)))
    probs = probs / lax.optimization_barrier(jnp.sum(probs, axis=-1, keepdims=True))
    local_out = jnp.einsum('hqk,khd->qhd', rounded(probs), block_values.astype(jnp.float32))
    cross = jnp.einsum('qhd,phd->hqp', queries_f, mem_keys.astype(jnp.float32)) * scale
    cross_probs = jnp.exp(cross - lax.optimization_barrier(jnp.max(cross, axis=-1, keepdims=True)))
    cross_probs = cross_probs / lax.optimization_barrier(jnp.sum(cross_probs, axis=-1, keepdims=True))
    cross_out = jnp.einsum('hqp,phd->qhd', rounded(cross_probs), mem_values.astype(jnp.float32))
    return (local_out + cross_out).astype(jnp.bfloat16)

def reference(tokens, w_query, w_key, w_value, w_out, slot_query, span_decay, ffn_up, ffn_down, norm_gain):
    queries = jnp.dot(tokens, w_query, preferred_element_type=jnp.float32).astype(jnp.bfloat16).reshape(TOKENS, ATTENDER_NUMBER, HS)
    keys_all = jnp.dot(tokens, w_key, preferred_element_type=jnp.float32).astype(jnp.bfloat16).reshape(TOKENS, ATTENDER_NUMBER, HS)
    values_all = jnp.dot(tokens, w_value, preferred_element_type=jnp.float32).astype(jnp.bfloat16).reshape(TOKENS, ATTENDER_NUMBER, HS)
    slots = slot_query.reshape(MEM, ATTENDER_NUMBER, HS).astype(jnp.float32)

    def pool(span):
        first_row = (span * CL).astype(jnp.int32)
        span_keys = lax.dynamic_slice_in_dim(keys_all, first_row, CL, 0)
        span_values = lax.dynamic_slice_in_dim(values_all, first_row, CL, 0)
        scores = jnp.einsum('phd,thd->hpt', slots, span_keys.astype(jnp.float32)) * HS ** (-0.5)
        peak_val = lax.optimization_barrier(jnp.max(scores, axis=-1))
        weights = jnp.exp(scores - peak_val[..., None])
        mass_sum = lax.optimization_barrier(jnp.sum(weights, axis=-1))
        weighted = jnp.einsum('hpt,thd->hpd', rounded(weights), span_values.astype(jnp.float32))
        return (peak_val, mass_sum, weighted)
    peaks, masses, pooled = lax.map(pool, jnp.arange(STRETCH_NUMBER, dtype=jnp.int32))
    identity = (jnp.zeros((ATTENDER_NUMBER,), jnp.float32), jnp.full((ATTENDER_NUMBER, MEM), floor_logit, jnp.float32), jnp.zeros((ATTENDER_NUMBER, MEM), jnp.float32), jnp.zeros((ATTENDER_NUMBER, MEM, HS), jnp.float32))

    def advance(running, element):
        return (merge_states(running, element), running)
    final_state, prefix = lax.scan(advance, identity, (span_decay, peaks, masses, pooled))
    memory = finish_memory(prefix).astype(jnp.bfloat16)
    memory = memory.transpose(0, 2, 1, 3).reshape(STRETCH_NUMBER * MEM, D)
    hidden = jax.nn.gelu(jnp.dot(memory, ffn_up, preferred_element_type=jnp.float32)).astype(jnp.bfloat16)
    settled = settle(memory, jnp.dot(hidden, ffn_down, preferred_element_type=jnp.float32), norm_gain)
    mem_keys = jnp.dot(settled, w_key, preferred_element_type=jnp.float32).astype(jnp.bfloat16).reshape(STRETCH_NUMBER, MEM, ATTENDER_NUMBER, HS)
    mem_values = jnp.dot(settled, w_value, preferred_element_type=jnp.float32).astype(jnp.bfloat16).reshape(STRETCH_NUMBER, MEM, ATTENDER_NUMBER, HS)
    padded_keys = jnp.concatenate([jnp.zeros((WIN, ATTENDER_NUMBER, HS), jnp.bfloat16), keys_all], 0)
    padded_values = jnp.concatenate([jnp.zeros((WIN, ATTENDER_NUMBER, HS), jnp.bfloat16), values_all], 0)
    blocks = CL // WIN

    def attend(index):
        span = index // blocks
        block_index = index % blocks
        first_row = (span * CL + block_index * WIN).astype(jnp.int32)
        block_queries = lax.dynamic_slice_in_dim(queries, first_row, WIN, 0)
        block_keys = lax.dynamic_slice_in_dim(padded_keys, first_row, 2 * WIN, 0)
        block_values = lax.dynamic_slice_in_dim(padded_values, first_row, 2 * WIN, 0)
        return window_block(block_queries, block_keys, block_values, WIN - first_row, mem_keys[span], mem_values[span])
    mixed = lax.map(attend, jnp.arange(STRETCH_NUMBER * blocks, dtype=jnp.int32)).reshape(TOKENS, D)
    return jnp.dot(mixed, w_out, preferred_element_type=jnp.float32).astype(jnp.bfloat16)
```

```python
import jax
import jax.numpy as jnp
from jax import lax
from jax.experimental import pallas as pl
from jax.experimental.pallas import tpu as pltpu
from jax.sharding import PartitionSpec as P

HS = 128
MEM = 64
NX, NY, NZ = 4, 4, 8
NG = NX * NY * NZ
HALF = 256
HC = 512
HEADS = 4
D = 1024
PART = MEM // NX
ROWS = HEADS * PART
FS = 512
MESH = pl.DeviceIdType.MESH
F32 = jnp.float32
BF = jnp.bfloat16
FLOOR = -1e30
NULL = 8.0
SCALE = HS ** (-0.5)
LOG2E = 1.4426950408889634


def nn(a, b):
    return lax.dot_general(a, b, (((1,), (0,)), ((), ())), preferred_element_type=F32)


def nt(a, b):
    return lax.dot_general(a, b, (((1,), (1,)), ((), ())), preferred_element_type=F32)


def merge(a, b):
    rate_a, peak_a, mass_a, val_a = a
    rate_b, peak_b, mass_b, val_b = b
    shifted = peak_a - rate_b
    high = jnp.maximum(shifted, peak_b)
    fa = jnp.exp(shifted - high)
    fb = jnp.exp(peak_b - high)
    return (rate_a + rate_b, high, mass_a * fa + mass_b * fb, val_a * fa + val_b * fb)


def pick(cond, a, b):
    return tuple(jnp.where(cond, p, q) for p, q in zip(a, b))


def identity():
    z = jnp.zeros((ROWS, 1), F32)
    return (z, z + FLOOR, z, jnp.zeros((ROWS, HS), F32))


def stat_columns(peak, mass, rate, rows):
    lane = lax.broadcasted_iota(jnp.int32, (rows, 128), 1)
    return jnp.where(lane == 0, peak, jnp.where(lane == 1, mass, jnp.where(lane == 2, rate, 0.0)))


def encode(state):
    rate, peak, mass, _ = state
    cols = stat_columns(peak, mass, rate, ROWS)
    full = jnp.concatenate([cols, jnp.zeros((128 - ROWS, 128), F32)], 0)
    return jnp.transpose(full)[0:8]


def decode(tiles, count):
    flat = tiles.reshape(count * 8, 128)
    full = jnp.concatenate([flat, jnp.zeros((128 - count * 8, 128), F32)], 0)
    return jnp.transpose(full)


def column_state(cols, k, val):
    return (cols[:, 8 * k + 2 : 8 * k + 3], cols[:, 8 * k : 8 * k + 1], cols[:, 8 * k + 1 : 8 * k + 2], val)


def body(
    tok_h, wq_h, wk_h, wv_h, wo_h, slot_ref, decay_ref, up_h, dn_h, gain_ref, out_ref,
    tok, ptok, wq, wk, wv, wo, qs, ks, vs, kp, vp, up, dn,
    ps, pst, sc, xr, xst, yr, yst, zr, zst, fm, pb, rs, own, st, lo, mk, mv, mx,
    load_sem, loc_sem, tok_s, tok_r, wx_s, wx_r, wz_s, wz_r, wy_s, wy_r,
    x_s, x_r, y_s, y_r, z_s, z_r, fm_s, fm_r, rs_s, rs_r, st_s, st_r, mx_s, mx_r,
):
    g = lax.axis_index("group")
    c = lax.axis_index("seq")
    x = lax.rem(g, NX)
    y = lax.rem(g // NX, NY)
    z = g // (NX * NY)
    oc = 1 - c

    def gid(zz, yy, xx):
        return zz * (NX * NY) + yy * NX + xx

    def xp(d):
        return lax.rem(x + d, NX)

    def yp(d):
        return lax.rem(y + d, NY)

    def zp(d):
        return lax.rem(z + d, NZ)

    nxt = lax.rem(g + 1, NG)
    prv = lax.rem(g + NG - 1, NG)
    sends = []

    def send(src, dst, ss, rsem, gg, cc):
        cp = pltpu.make_async_remote_copy(
            src_ref=src, dst_ref=dst, send_sem=ss, recv_sem=rsem,
            device_id={"group": gg, "seq": cc}, device_id_type=MESH,
        )
        cp.start()
        sends.append(cp)
        return cp

    def arrived(ref, sem, ss):
        pltpu.make_async_remote_copy(
            src_ref=ref, dst_ref=ref, send_sem=ss, recv_sem=sem,
            device_id={"group": g, "seq": oc}, device_id_type=MESH,
        ).wait_recv()

    loads = []
    for k, (src, dst) in enumerate(
        ((tok_h, tok.at[c]), (wk_h, wk), (wv_h, wv), (wq_h, wq), (wo_h, wo))
    ):
        cp = pltpu.make_async_copy(src, dst, load_sem.at[k])
        cp.start()
        loads.append(cp)
    lanes_x = pl.ds(pl.multiple_of(x * FS, FS), FS)
    wl = []
    for k, (src, dst) in enumerate(((up_h, up), (dn_h, dn))):
        cp = pltpu.make_async_copy(src.at[:, lanes_x], dst.at[z, y, x], loc_sem.at[k])
        cp.start()
        wl.append(cp)

    barrier = pltpu.get_barrier_semaphore()

    def greet(gg, cc):
        pl.semaphore_signal(barrier, inc=1, device_id={"group": gg, "seq": cc}, device_id_type=MESH)

    greet(g, oc)
    for d in range(1, NX):
        greet(gid(z, y, xp(d)), c)
        greet(gid(z, y, xp(d)), oc)
    for d in range(1, NY):
        greet(gid(z, yp(d), x), c)
    for d in range(1, NZ):
        greet(gid(zp(d), y, x), c)
    greet(nxt, c)
    greet(prv, c)

    def project(half):
        rows = tok[half]
        ks[half] = nn(rows, wk[...]).astype(BF)
        vs[half] = nn(rows, wv[...]).astype(BF)
        qs[half] = nn(rows, wq[...]).astype(BF)

    pl.semaphore_wait(barrier, 2 * (NX - 1) + (NY - 1) + (NZ - 1) + 3)

    send(tok_h, tok.at[c], tok_s.at[0], tok_r.at[0], g, oc)
    for k, (src, dst) in enumerate(((up_h, up), (dn_h, dn))):
        for d in range(1, NX):
            to = xp(d)
            send(
                src.at[:, pl.ds(pl.multiple_of(to * FS, FS), FS)], dst.at[z, y, x],
                wx_s.at[k, d - 1], wx_r.at[k, d - 1], gid(z, y, to), c,
            )
    send(tok_h, ptok.at[c], tok_s.at[1], tok_r.at[1], nxt, c)

    for cp in loads[:4]:
        cp.wait()
    project(c)

    def weights_z(k, buf):
        wl[k].wait()
        for d in range(1, NX):
            arrived(buf.at[z, y, xp(NX - d)], wx_r.at[k, d - 1], wx_s.at[k, d - 1])
        for d in range(1, NZ):
            send(
                buf.at[z, y], buf.at[z, y], wz_s.at[k, d - 1], wz_r.at[k, d - 1],
                gid(zp(d), y, x), c,
            )

    def weights_y(k, buf):
        for d in range(1, NZ):
            arrived(buf.at[zp(NZ - d), y], wz_r.at[k, d - 1], wz_s.at[k, d - 1])
        for d in range(1, NY):
            send(
                buf.at[:, y], buf.at[:, y], wy_s.at[k, d - 1], wy_r.at[k, d - 1],
                gid(z, yp(d), x), c,
            )

    def weights_done(k, buf):
        for d in range(1, NY):
            arrived(buf.at[:, yp(NY - d)], wy_r.at[k, d - 1], wy_s.at[k, d - 1])

    weights_z(0, up)
    weights_z(1, dn)

    arrived(tok.at[oc], tok_r.at[0], tok_s.at[0])
    project(oc)

    for h in range(HEADS):
        cols = slice(h * HS, (h + 1) * HS)
        keys = ks[:, :, cols].reshape(2 * HALF, HS)
        vals = vs[:, :, cols].reshape(2 * HALF, HS)
        scores = nt(slot_ref[:, cols], keys) * SCALE
        peak = jnp.max(scores, axis=1, keepdims=True)
        w = jnp.exp(scores - peak)
        mass = jnp.sum(w, axis=1, keepdims=True)
        pooled = nn(w.astype(BF), vals)
        stat = stat_columns(peak, mass, decay_ref[0:1, h : h + 1], MEM)
        for p in range(NX):
            rows = slice(p * PART, (p + 1) * PART)
            ps[p, h * PART : (h + 1) * PART, :] = pooled[rows]
            first = (p % 2) * ROWS + h * PART
            sc[p // 2, first : first + PART, :] = stat[rows]
    for q in range(2):
        pst[q] = jnp.transpose(sc[q])[0:8]

    for d in range(1, NX):
        to = xp(d)
        send(ps.at[to], xr.at[x], x_s.at[0, d - 1], x_r.at[0, d - 1], gid(z, y, to), c)
        send(pst.at[to // 2], xst.at[x], x_s.at[1, d - 1], x_r.at[1, d - 1], gid(z, y, to), c)
    xr[x] = ps[x]
    xst[x] = pst[x // 2]
    for d in range(1, NX):
        frm = xp(NX - d)
        arrived(xr.at[frm], x_r.at[0, d - 1], x_s.at[0, d - 1])
        arrived(xst.at[frm], x_r.at[1, d - 1], x_s.at[1, d - 1])
    both = decode(xst[...], NX)
    cols = jnp.where(lax.rem(x, 2) == 0, both[0:ROWS], both[ROWS : 2 * ROWS])
    in_row = [identity()]
    total = column_state(cols, 0, xr[0])
    for j in range(1, NX):
        in_row.append(total)
        total = merge(total, column_state(cols, j, xr[j]))

    yr[y] = total[3]
    yst[y] = encode(total)
    for d in range(1, NY):
        to = gid(z, yp(d), x)
        send(yr.at[y], yr.at[y], y_s.at[0, d - 1], y_r.at[0, d - 1], to, c)
        send(yst.at[y], yst.at[y], y_s.at[1, d - 1], y_r.at[1, d - 1], to, c)
    for d in range(1, NY):
        frm = yp(NY - d)
        arrived(yr.at[frm], y_r.at[0, d - 1], y_s.at[0, d - 1])
        arrived(yst.at[frm], y_r.at[1, d - 1], y_s.at[1, d - 1])
    cols = decode(yst[...], NY)[0:ROWS]
    in_plane = identity()
    total = None
    for j in range(NY):
        item = column_state(cols, j, yr[j])
        in_plane = pick(j < y, merge(in_plane, item), in_plane)
        total = item if total is None else merge(total, item)

    zr[z] = total[3]
    zst[z] = encode(total)
    for d in range(1, NZ):
        to = gid(zp(d), y, x)
        send(zr.at[z], zr.at[z], z_s.at[0, d - 1], z_r.at[0, d - 1], to, c)
        send(zst.at[z], zst.at[z], z_s.at[1, d - 1], z_r.at[1, d - 1], to, c)

    arrived(ptok.at[c], tok_r.at[1], tok_s.at[1])
    send(ptok.at[c], ptok.at[c], tok_s.at[2], tok_r.at[2], g, oc)

    def project_prev(half):
        rows = ptok[half]
        kp[half] = nn(rows, wk[...]).astype(BF)
        vp[half] = nn(rows, wv[...]).astype(BF)

    project_prev(c)
    weights_y(0, up)
    weights_y(1, dn)
    arrived(ptok.at[oc], tok_r.at[2], tok_s.at[2])
    project_prev(oc)

    row_i = lax.broadcasted_iota(jnp.int32, (HALF, HALF), 0)
    col_i = lax.broadcasted_iota(jnp.int32, (HALF, HALF), 1)
    tri = col_i <= row_i
    bias = jnp.where(g == 0, FLOOR, 0.0).astype(F32)

    def attend(h, i):
        cols = slice(h * HS, (h + 1) * HS)
        q = qs[i, :, cols]
        near = nt(q, ks[i, :, cols])
        far = nt(q, kp[i, :, cols]) + bias
        diag = jnp.where(tri, near, far)
        if i == 0:
            full = nt(q, kp[1, :, cols]) + bias
            full_v = vp[1, :, cols]
        else:
            full = nt(q, ks[0, :, cols])
            full_v = vs[0, :, cols]
        high = jnp.maximum(
            jnp.max(diag, axis=1, keepdims=True), jnp.max(full, axis=1, keepdims=True)
        )
        ed = jnp.exp2((diag - high) * (SCALE * LOG2E))
        ef = jnp.exp2((full - high) * (SCALE * LOG2E))
        mass = jnp.sum(ed, axis=1, keepdims=True) + jnp.sum(ef, axis=1, keepdims=True)
        acc = nn(jnp.where(tri, ed, 0.0).astype(BF), vs[i, :, cols])
        acc += nn(jnp.where(tri, 0.0, ed).astype(BF), vp[i, :, cols])
        acc += nn(ef.astype(BF), full_v)
        lo[i, :, cols] = acc / mass

    for h in range(HEADS):
        for i in range(2):
            attend(h, i)

    for d in range(1, NZ):
        frm = zp(NZ - d)
        arrived(zr.at[frm], z_r.at[0, d - 1], z_s.at[0, d - 1])
        arrived(zst.at[frm], z_r.at[1, d - 1], z_s.at[1, d - 1])
    cols = decode(zst[...], NZ)[0:ROWS]
    before = identity()
    for j in range(NZ):
        before = pick(j < z, merge(before, column_state(cols, j, zr[j])), before)
    before = merge(before, in_plane)
    for j in range(NX):
        _, peak, mass, val = merge(before, in_row[j])
        anchor = jnp.maximum(peak, NULL)
        factor = jnp.exp(peak - anchor)
        denom = mass * factor + jnp.exp(NULL - anchor)
        memory = (val * (factor / denom)).astype(BF)
        for h in range(HEADS):
            fm[c, x, j * PART : (j + 1) * PART, h * HS : (h + 1) * HS] = memory[
                h * PART : (h + 1) * PART
            ]
    k = 0
    row_peers = [(0, True)] + [(d, f) for d in range(1, NX) for f in (False, True)]
    for d, flip in row_peers:
        send(
            fm.at[c, x], fm.at[c, x], fm_s.at[k], fm_r.at[k],
            gid(z, y, xp(d)), oc if flip else c,
        )
        k += 1
    k = 0
    for d, flip in row_peers:
        arrived(fm.at[oc if flip else c, xp(NX - d) if d else x], fm_r.at[k], fm_s.at[k])
        k += 1

    weights_done(0, up)
    mem0 = fm[0].reshape(NX * MEM, HC)
    mem1 = fm[1].reshape(NX * MEM, HC)
    total = nn(mem0, up[0 : NZ // 2].reshape(D // 2, FS)) + nn(mem1, up[NZ // 2 :].reshape(D // 2, FS))
    hidden = jax.nn.gelu(total, approximate=True).astype(BF)
    weights_done(1, dn)
    part = nt(hidden, dn[...].reshape(D, FS))
    for j in range(NX):
        for cc in range(2):
            for q in range(2):
                first = (2 * cc + q) * MEM + j * PART
                piece = part[first : first + PART]
                own[j, cc, q * PART : (q + 1) * PART, :] = piece
                pb[j, cc, q * PART : (q + 1) * PART, :] = piece.astype(BF)
    k = 0
    for d, flip in row_peers:
        to = xp(d)
        cc = oc if flip else c
        send(pb.at[to, cc], rs.at[k], rs_s.at[k], rs_r.at[k], gid(z, y, to), cc)
        k += 1
    acc = own[x, c]
    mem = fm[:, pl.ds(2 * c, 2), pl.ds(pl.multiple_of(x * PART, PART), PART), :]
    mem = jnp.concatenate(
        [mem[0].reshape(2 * PART, HC), mem[1].reshape(2 * PART, HC)], 1
    ).astype(F32)
    for k in range(7):
        arrived(rs.at[k], rs_r.at[k], rs_s.at[k])
    for k in range(7):
        acc += rs[k].astype(F32)
    summed = mem + acc
    scaled = summed * lax.rsqrt(jnp.mean(summed * summed, axis=-1, keepdims=True) + 1e-06)
    st[c] = (scaled * gain_ref[...]).astype(BF)
    send(st.at[c], st.at[c], st_s, st_r, g, oc)
    arrived(st.at[oc], st_r, st_s)
    settled = st[...].reshape(MEM, D)
    mk[...] = nn(settled, wk[...]).astype(BF)
    mv[...] = nn(settled, wv[...]).astype(BF)

    for h in range(HEADS):
        cols = slice(h * HS, (h + 1) * HS)
        q = qs[:, :, cols].reshape(2 * HALF, HS)
        scores = nt(q, mk[:, cols])
        high = jnp.max(scores, axis=1, keepdims=True)
        e = jnp.exp2((scores - high) * (SCALE * LOG2E))
        probs = (e / jnp.sum(e, axis=1, keepdims=True)).astype(BF)
        cross = nn(probs, mv[:, cols])
        both = lo[:, :, cols].reshape(2 * HALF, HS) + cross
        mx[c, h] = both.astype(BF)
        send(mx.at[c, h], mx.at[c, h], mx_s.at[h], mx_r.at[h], g, oc)
    loads[4].wait()

    def out_part(cc, h):
        return nn(mx[cc, h], wo[pl.ds(pl.multiple_of(cc * HC + h * HS, HS), HS), :])

    acc = out_part(c, 0)
    for h in range(1, HEADS):
        acc += out_part(c, h)
    for h in range(HEADS):
        arrived(mx.at[oc, h], mx_r.at[h], mx_s.at[h])
        acc += out_part(oc, h)
    out_ref[...] = acc.astype(BF)

    for cp in sends:
        cp.wait_send()


def shards(tokens, w_query, w_key, w_value, w_out, slot_query, span_decay, ffn_up, ffn_down, norm_gain):
    V = pltpu.VMEM
    DMA = pltpu.SemaphoreType.DMA
    scratch = [
        V((2, HALF, D), BF), V((2, HALF, D), BF),
        V((D, HC), BF), V((D, HC), BF), V((D, HC), BF), V((D, HC), BF),
        V((2, HALF, HC), BF), V((2, HALF, HC), BF), V((2, HALF, HC), BF),
        V((2, HALF, HC), BF), V((2, HALF, HC), BF),
        V((NZ, NY, NX, 8, FS), BF), V((NZ, NY, NX, 8, FS), BF),
        V((NX, ROWS, HS), F32), V((2, 8, 128), F32), V((2, 128, 128), F32),
        V((NX, ROWS, HS), F32), V((NX, 8, 128), F32),
        V((NY, ROWS, HS), F32), V((NY, 8, 128), F32),
        V((NZ, ROWS, HS), F32), V((NZ, 8, 128), F32),
        V((2, NX, NX * PART, HC), BF),
        V((NX, 2, 2 * PART, D), BF), V((7, 2 * PART, D), BF), V((NX, 2, 2 * PART, D), F32),
        V((2, 2 * PART, D), BF),
        V((2, HALF, HC), F32),
        V((MEM, HC), BF), V((MEM, HC), BF),
        V((2, HEADS, 2 * HALF, HS), BF),
        DMA((5,)), DMA((2,)), DMA((3,)), DMA((3,)),
        DMA((2, NX - 1)), DMA((2, NX - 1)), DMA((2, NZ - 1)), DMA((2, NZ - 1)),
        DMA((2, NY - 1)), DMA((2, NY - 1)),
        DMA((2, NX - 1)), DMA((2, NX - 1)), DMA((2, NY - 1)), DMA((2, NY - 1)),
        DMA((2, NZ - 1)), DMA((2, NZ - 1)),
        DMA((7,)), DMA((7,)), DMA((7,)), DMA((7,)), DMA, DMA, DMA((HEADS,)), DMA((HEADS,)),
    ]
    hbm = pl.BlockSpec(memory_space=pl.ANY)
    vm = pl.BlockSpec(memory_space=pltpu.VMEM)
    return pl.pallas_call(
        body,
        out_shape=jax.ShapeDtypeStruct((2 * HALF, HC), BF),
        in_specs=[hbm, hbm, hbm, hbm, hbm, vm, vm, hbm, hbm, vm],
        out_specs=vm,
        scratch_shapes=scratch,
        compiler_params=pltpu.CompilerParams(
            collective_id=0, has_side_effects=True, vmem_limit_bytes=60 * 1024 * 1024
        ),
    )(
        tokens, w_query, w_key, w_value, w_out, slot_query, span_decay, ffn_up,
        ffn_down.T, norm_gain.reshape(1, D),
    )


def solution(mesh):
    in_specs = (
        P(("group", "seq"), None),
        P(None, "seq"),
        P(None, "seq"),
        P(None, "seq"),
        P(None, "seq"),
        P(None, "seq"),
        P("group", "seq"),
        P("group", "seq"),
        P("seq", "group"),
        P(),
    )
    out_specs = P("group", "seq")
    return jax.shard_map(shards, mesh=mesh, in_specs=in_specs, out_specs=out_specs, check_vma=False)
```

```python
import jax
import jax.numpy as jnp
from jax import lax
from jax.experimental import pallas as pl
from jax.experimental.pallas import tpu as pltpu
from jax.sharding import PartitionSpec as P

HS = 128
MEM = 64
NX, NY, NZ = 4, 4, 8
NG = NX * NY * NZ
HALF = 256
HC = 512
HEADS = 4
D = 1024
PART = MEM // NX
ROWS = HEADS * PART
FS = 512
TAILS = 4
FORWARD = (1, 3, 2)
MESH = pl.DeviceIdType.MESH
F32 = jnp.float32
BF = jnp.bfloat16
FLOOR = -1e30
NULL = 8.0
SCALE = HS ** (-0.5)
LOG2E = 1.4426950408889634


def nn(a, b):
    return lax.dot_general(a, b, (((1,), (0,)), ((), ())), preferred_element_type=F32)


def nt(a, b):
    return lax.dot_general(a, b, (((1,), (1,)), ((), ())), preferred_element_type=F32)


def stat_columns(peak, mass, rate, rows):
    lane = lax.broadcasted_iota(jnp.int32, (rows, 128), 1)
    return jnp.where(lane == 0, peak, jnp.where(lane == 1, mass, jnp.where(lane == 2, rate, 0.0)))


def before_item(items, stop):
    rate = jnp.zeros_like(items[0][0])
    shifted = [None] * len(items)
    for k in reversed(range(len(items))):
        live = k < stop
        shifted[k] = jnp.where(live, items[k][0] - rate, FLOOR)
        rate = rate + jnp.where(live, items[k][2], 0.0)
    peak = shifted[0]
    for a in shifted[1:]:
        peak = jnp.maximum(peak, a)
    weights = [jnp.where(k < stop, jnp.exp(a - peak), 0.0) for k, a in enumerate(shifted)]
    mass = jnp.zeros_like(rate)
    for w, item in zip(weights, items):
        mass = mass + item[1] * w
    return (peak, mass, rate), weights


def weighted(cols, first, values):
    total = cols[:, first : first + 1] * values[0].astype(F32)
    for k in range(1, len(values)):
        total = total + cols[:, first + k : first + k + 1] * values[k].astype(F32)
    return total


def body(
    tok_h, wq_h, wk_h, wv_h, wo_h, slot_ref, decay_ref, up_h, dn_h, gain_ref, out_ref,
    tok, ptok, wq, wk, wv, wo, qs, ks, vs, kp, vp, ff,
    ps, pst, sc, xr, xst, yr, yst, zr, zst, fm, pb, rs, own, pc, pc_in, hid, st, lo, mk, mv, mx,
    tr, relay, load_sem, loc_sem, tok_s, tok_r, tail_s, tail_r, relay_s, relay_r, wx_s, wx_r, rg_s, rg_r, ny_s, ny_r, fy_s, fy_r,
    x_s, x_r, y_s, y_r, z_s, z_r, fm_s, fm_r, rs_s, rs_r, st_s, st_r, mx_s, mx_r,
):
    g = lax.axis_index("group")
    c = lax.axis_index("seq")
    x = lax.rem(g, NX)
    y = lax.rem(g // NX, NY)
    z = g // (NX * NY)
    oc = 1 - c

    def gid(zz, yy, xx):
        return zz * (NX * NY) + yy * NX + xx

    def xp(d):
        return lax.rem(x + d, NX)

    def yp(d):
        return lax.rem(y + d, NY)

    def zp(d):
        return lax.rem(z + d, NZ)

    nxt = lax.rem(g + 1, NG)
    prv = lax.rem(g + NG - 1, NG)
    down_row, up_row = lax.rem(g + NX, NG), lax.rem(g + NG - NX, NG)
    sends = []

    def send(src, dst, ss, rsem, gg, cc):
        cp = pltpu.make_async_remote_copy(
            src_ref=src, dst_ref=dst, send_sem=ss, recv_sem=rsem,
            device_id={"group": gg, "seq": cc}, device_id_type=MESH,
        )
        cp.start()
        sends.append(cp)
        return cp

    def arrived(ref, sem, ss):
        pltpu.make_async_remote_copy(
            src_ref=ref, dst_ref=ref, send_sem=ss, recv_sem=sem,
            device_id={"group": g, "seq": oc}, device_id_type=MESH,
        ).wait_recv()

    loads = []
    for k, (src, dst) in enumerate(
        ((tok_h, tok.at[c]), (wk_h, wk), (wv_h, wv), (wq_h, wq), (wo_h, wo))
    ):
        cp = pltpu.make_async_copy(src, dst, load_sem.at[k])
        cp.start()
        loads.append(cp)
    lanes_x = pl.ds(pl.multiple_of(x * FS, FS), FS)
    wl = []
    for k, (src, dst) in enumerate(((up_h, ff), (dn_h, ff))):
        cp = pltpu.make_async_copy(src.at[:, lanes_x], dst.at[z, y, k, x], loc_sem.at[k])
        cp.start()
        wl.append(cp)

    tr[...] = jnp.zeros_like(tr)
    barrier = pltpu.get_barrier_semaphore()

    def greet(gg, cc):
        pl.semaphore_signal(barrier, inc=1, device_id={"group": gg, "seq": cc}, device_id_type=MESH)

    greet(g, oc)
    for d in range(1, NX):
        greet(gid(z, y, xp(d)), c)
        greet(gid(z, y, xp(d)), oc)
    for d in range(1, NY):
        greet(gid(z, yp(d), x), c)
    for d in range(1, NZ):
        greet(gid(zp(d), y, x), c)
    greet(nxt, c)
    greet(prv, c)
    greet(down_row, c)
    greet(up_row, c)

    def project(half):
        rows = tok[half]
        ks[half] = nn(rows, wk[...]).astype(BF)
        vs[half] = nn(rows, wv[...]).astype(BF)

    pl.semaphore_wait(barrier, 2 * (NX - 1) + (NY - 1) + (NZ - 1) + 5)

    send(tok_h, tok.at[c], tok_s.at[0], tok_r.at[0], g, oc)
    for k, (src, dst) in enumerate(((up_h, ff), (dn_h, ff))):
        for d in range(1, NX):
            to = xp(d)
            send(
                src.at[:, pl.ds(pl.multiple_of(to * FS, FS), FS)], dst.at[z, y, k, x],
                wx_s.at[k, d - 1], wx_r.at[k, d - 1], gid(z, y, to), c,
            )

    row_end, row_start = x == NX - 1, x == 0
    tails, handed, relayed = [], [], []
    for k in range(TAILS):
        rows = slice(k * (HALF // TAILS), (k + 1) * (HALF // TAILS))

        def piece(src, dst, ss, rsem, to):
            return pltpu.make_async_remote_copy(
                src_ref=src, dst_ref=dst, send_sem=ss, recv_sem=rsem,
                device_id={"group": to, "seq": c}, device_id_type=MESH,
            )

        there = ptok.at[c, rows]
        tails.append(piece(tok_h.at[rows], there, tail_s.at[k], tail_r.at[k], nxt))
        handed.append(
            piece(tok_h.at[rows], relay.at[k], tail_s.at[k], relay_r.at[k], gid(z, y, 0))
        )
        relayed.append(piece(relay.at[k], there, relay_s.at[k], tail_r.at[k], down_row))
    sends.extend(tails)

    def tail_start(k, cond):
        pl.when(cond)(tails[k].start)

    def relay_start(k, cond):
        @pl.when(row_start & cond)
        def _():
            handed[k].wait_recv()
            relayed[k].start()

    tail_start(0, x == NX - 1)
    for cp in loads[:3]:
        cp.wait()
    project(c)

    left_y, right_y = yp(NY - 1), yp(1)
    left_z, right_z = zp(NZ - 1), zp(1)

    def weights_x():
        for k in range(2):
            wl[k].wait()
            for d in range(1, NX):
                arrived(ff.at[z, y, k, xp(NX - d)], wx_r.at[k, d - 1], wx_s.at[k, d - 1])

    def weights_ring(step):
        a, b = ff.at[zp(NZ + 1 - step), y], ff.at[zp(step - 1), y]
        if step == NZ // 2:
            a, b = a.at[0], b.at[1]
        send(a, a, rg_s.at[0, step - 1], rg_r.at[0, step - 1], gid(right_z, y, x), c)
        send(b, b, rg_s.at[1, step - 1], rg_r.at[1, step - 1], gid(left_z, y, x), c)

    def ring_wait(step):
        a, b = ff.at[zp(NZ - step), y], ff.at[zp(step), y]
        if step == NZ // 2:
            a, b = a.at[0], b.at[1]
        arrived(a, rg_r.at[0, step - 1], rg_s.at[0, step - 1])
        arrived(b, rg_r.at[1, step - 1], rg_s.at[1, step - 1])

    def weights_near(o):
        b = ff.at[zp(o), y]
        send(b, b, ny_s.at[0, o], ny_r.at[0, o], gid(z, right_y, x), c)
        send(b, b, ny_s.at[1, o], ny_r.at[1, o], gid(z, left_y, x), c)

    def weights_far(o):
        from_left = ff.at[zp(o), left_y]
        from_right = ff.at[zp(o), right_y]
        arrived(from_left, ny_r.at[0, o], ny_s.at[0, o])
        arrived(from_right, ny_r.at[1, o], ny_s.at[1, o])
        if o < NZ // 4:
            src, to = left_y, right_y
        elif o < NZ // 2:
            src = jnp.where(x == 0, right_y, left_y)
            to = jnp.where(x == 0, left_y, right_y)
        else:
            src, to = right_y, left_y
        b = ff.at[zp(o), src]
        send(b, b, fy_s.at[o], fy_r.at[o], gid(z, to, x), c)

    def weights_done():
        for o in range(NZ):
            arrived(ff.at[zp(o), yp(2)], fy_r.at[o], fy_s.at[o])

    arrived(tok.at[oc], tok_r.at[0], tok_s.at[0])
    project(oc)

    for h in range(HEADS):
        cols = slice(h * HS, (h + 1) * HS)
        keys = ks[:, :, cols].reshape(2 * HALF, HS)
        vals = vs[:, :, cols].reshape(2 * HALF, HS)
        scores = nt(slot_ref[:, cols], keys) * SCALE
        peak = jnp.max(scores, axis=1, keepdims=True)
        w = jnp.exp(scores - peak)
        mass = jnp.sum(w, axis=1, keepdims=True)
        pooled = nn(w.astype(BF), vals)
        stat = stat_columns(peak, mass, decay_ref[0:1, h : h + 1], MEM)
        for p in range(NX):
            rows = slice(p * PART, (p + 1) * PART)
            ps[p, h * PART : (h + 1) * PART, :] = pooled[rows].astype(BF)
            first = (p % 2) * ROWS + h * PART
            sc[p // 2, first : first + PART, :] = stat[rows]
    for q in range(2):
        pst[q] = jnp.transpose(sc[q])[0:8]

    for d in range(1, NX):
        to = xp(d)
        send(ps.at[to], xr.at[x], x_s.at[0, d - 1], x_r.at[0, d - 1], gid(z, y, to), c)
        send(pst.at[to // 2], xst.at[x], x_s.at[1, d - 1], x_r.at[1, d - 1], gid(z, y, to), c)
    for k in range(TAILS):
        tail_start(k, x < NX - 1)
        if k:
            pl.when(row_end)(handed[k].start)
    xr[x] = ps[x]
    xst[x] = pst[x // 2]
    weights_x()
    weights_ring(1)
    weights_near(0)
    loads[3].wait()
    for half in range(2):
        qs[half] = nn(tok[half], wq[...]).astype(BF)
    for d in range(1, NX):
        frm = xp(NX - d)
        arrived(xr.at[frm], x_r.at[0, d - 1], x_s.at[0, d - 1])
        arrived(xst.at[frm], x_r.at[1, d - 1], x_s.at[1, d - 1])
    odd = lax.rem(x, 2) == 1
    items = []
    for k in range(NX):
        tile = xst[k]
        tile = jnp.where(odd, pltpu.roll(tile, 64, 1), tile)
        items.append(tuple(tile[r : r + 1] for r in range(3)))
    in_row = [before_item(items, j) for j in range(NX + 1)]
    n = 0
    for j in range(1, NX + 1):
        for k in range(j):
            tr[n : n + 1] = in_row[j][1][k]
            n += 1
    cols = jnp.transpose(tr[...])[0:ROWS]
    row_val = [None]
    n = 0
    for j in range(1, NX + 1):
        row_val.append(weighted(cols, n, [xr[k] for k in range(j)]))
        n += j

    def stat_tile(state):
        sub = lax.broadcasted_iota(jnp.int32, (8, 128), 0)
        return jnp.where(sub == 0, state[0], jnp.where(sub == 1, state[1], state[2]))

    yr[y] = row_val[NX].astype(BF)
    yst[y] = stat_tile(in_row[NX][0])
    for d in range(1, NY):
        to = gid(z, yp(d), x)
        send(yr.at[y], yr.at[y], y_s.at[0, d - 1], y_r.at[0, d - 1], to, c)
        send(yst.at[y], yst.at[y], y_s.at[1, d - 1], y_r.at[1, d - 1], to, c)
    ring_wait(1)
    weights_ring(2)
    weights_near(1)
    weights_near(NZ - 1)
    for d in range(1, NY):
        frm = yp(NY - d)
        arrived(yr.at[frm], y_r.at[0, d - 1], y_s.at[0, d - 1])
        arrived(yst.at[frm], y_r.at[1, d - 1], y_s.at[1, d - 1])
    items = [tuple(yst[k, r : r + 1] for r in range(3)) for k in range(NY)]
    in_plane, w_some = before_item(items, y)
    plane, w_all = before_item(items, NY)
    for k in range(NY):
        tr[k : k + 1] = w_all[k]
        tr[NY + k : NY + k + 1] = w_some[k]
    cols = jnp.transpose(tr[...])[0:ROWS]
    vals = [yr[k] for k in range(NY)]

    zr[z] = weighted(cols, 0, vals).astype(BF)
    zst[z] = stat_tile(plane)
    for d in range(1, NZ):
        to = gid(zp(d), y, x)
        send(zr.at[z], zr.at[z], z_s.at[0, d - 1], z_r.at[0, d - 1], to, c)
        send(zst.at[z], zst.at[z], z_s.at[1, d - 1], z_r.at[1, d - 1], to, c)
    plane_val = weighted(cols, NY, vals)
    ring_wait(2)
    weights_ring(3)
    weights_near(2)
    weights_near(NZ - 2)
    weights_far(0)
    weights_far(1)
    weights_far(NZ - 1)
    relay_start(1, y < NY - 1)
    for d in range(1, NZ):
        frm = zp(NZ - d)
        arrived(zr.at[frm], z_r.at[0, d - 1], z_s.at[0, d - 1])
        arrived(zst.at[frm], z_r.at[1, d - 1], z_s.at[1, d - 1])
    items = [tuple(zst[k, r : r + 1] for r in range(3)) for k in range(NZ)]
    planes, w_some = before_item(items, z)
    for k in range(NZ):
        tr[k : k + 1] = w_some[k]
    n = NZ
    for j in range(NX):
        own_peak, own_mass, own_rate = in_row[j][0]
        shifted = [planes[0] - in_plane[2] - own_rate, in_plane[0] - own_rate, own_peak]
        peak = jnp.maximum(jnp.maximum(shifted[0], shifted[1]), shifted[2])
        parts = [jnp.exp(a - peak) for a in shifted]
        mass = planes[1] * parts[0] + in_plane[1] * parts[1] + own_mass * parts[2]
        anchor = jnp.maximum(peak, NULL)
        factor = jnp.exp(peak - anchor)
        coef = factor / (mass * factor + jnp.exp(NULL - anchor))
        for part in parts:
            tr[n : n + 1] = part * coef
            n += 1
    cols = jnp.transpose(tr[...])[0:ROWS]
    planes_val = weighted(cols, 0, [zr[k] for k in range(NZ)])
    for j in range(NX):
        vals = [planes_val, plane_val] + ([row_val[j]] if j else [])
        memory = weighted(cols, NZ + 3 * j, vals).astype(BF)
        for h in range(HEADS):
            fm[c, x, j * PART : (j + 1) * PART, h * HS : (h + 1) * HS] = memory[
                h * PART : (h + 1) * PART
            ]
    b = fm.at[c, x]
    for d in range(1, NX):
        send(b, b, fm_s.at[0, d], fm_r.at[0, d], gid(z, y, xp(d)), c)
    send(b, b, fm_s.at[1, 0], fm_r.at[1, 0], g, oc)
    weights_far(2)
    weights_far(NZ - 2)
    ring_wait(3)
    weights_ring(4)
    weights_near(3)
    weights_near(NZ - 3)
    relay_start(1, y == NY - 1)
    ring_wait(NZ // 2)
    weights_near(NZ // 2)
    for d in FORWARD:
        b = fm.at[c, xp(NX - d)]
        arrived(b, fm_r.at[0, d], fm_s.at[0, d])
        send(b, b, fm_s.at[1, d], fm_r.at[1, d], g, oc)
    weights_far(3)
    weights_far(NZ - 3)
    weights_far(NZ // 2)
    relay_start(2, True)
    relay_start(3, True)
    arrived(fm.at[oc, x], fm_r.at[1, 0], fm_s.at[1, 0])
    for d in FORWARD:
        arrived(fm.at[oc, xp(NX - d)], fm_r.at[1, d], fm_s.at[1, d])
    weights_done()
    up = ff[:, :, 0].reshape(D, FS)
    total = nn(fm[0].reshape(NX * MEM, HC), up[0:HC]) + nn(fm[1].reshape(NX * MEM, HC), up[HC:])
    hid[...] = jax.nn.gelu(total, approximate=True).astype(BF).reshape(2, 2 * MEM, FS)
    down = ff[:, :, 1].reshape(D, FS)
    pc[...] = nt(hid[oc], down).astype(BF)
    send(pc, pc_in, rs_s.at[0], rs_r.at[0], g, oc)
    own[...] = nt(hid[c], down)
    arrived(pc_in, rs_r.at[0], rs_s.at[0])
    own[...] += pc_in[...].astype(F32)
    for j in range(NX):
        for q in range(2):
            first = q * MEM + j * PART
            pb[j, q * PART : (q + 1) * PART, :] = own[first : first + PART].astype(BF)
    for d in FORWARD:
        to = xp(d)
        send(pb.at[to], rs.at[d - 1], rs_s.at[d], rs_r.at[d], gid(z, y, to), c)
    for cp in tails:
        cp.wait_recv()
    send(ptok.at[c], ptok.at[c], tok_s.at[1], tok_r.at[1], g, oc)

    def project_prev(half):
        rows = ptok[half]
        kp[half] = nn(rows, wk[...]).astype(BF)
        vp[half] = nn(rows, wv[...]).astype(BF)

    project_prev(c)
    arrived(ptok.at[oc], tok_r.at[1], tok_s.at[1])
    project_prev(oc)

    row_i = lax.broadcasted_iota(jnp.int32, (HALF, HALF), 0)
    col_i = lax.broadcasted_iota(jnp.int32, (HALF, HALF), 1)
    tri = col_i <= row_i
    bias = jnp.where(g == 0, FLOOR, 0.0).astype(F32)

    def attend(h, i):
        cols = slice(h * HS, (h + 1) * HS)
        q = qs[i, :, cols]
        near = nt(q, ks[i, :, cols])
        far = nt(q, kp[i, :, cols]) + bias
        diag = jnp.where(tri, near, far)
        if i == 0:
            full = nt(q, kp[1, :, cols]) + bias
            full_v = vp[1, :, cols]
        else:
            full = nt(q, ks[0, :, cols])
            full_v = vs[0, :, cols]
        high = jnp.maximum(
            jnp.max(diag, axis=1, keepdims=True), jnp.max(full, axis=1, keepdims=True)
        )
        ed = jnp.exp2((diag - high) * (SCALE * LOG2E))
        ef = jnp.exp2((full - high) * (SCALE * LOG2E))
        mass = jnp.sum(ed, axis=1, keepdims=True) + jnp.sum(ef, axis=1, keepdims=True)
        acc = nn(jnp.where(tri, ed, 0.0).astype(BF), vs[i, :, cols])
        acc += nn(jnp.where(tri, 0.0, ed).astype(BF), vp[i, :, cols])
        acc += nn(ef.astype(BF), full_v)
        lo[i, :, cols] = acc / mass

    for h in range(HEADS):
        for i in range(2):
            attend(h, i)
    for d in FORWARD:
        arrived(rs.at[d - 1], rs_r.at[d], rs_s.at[d])
    mine = pl.ds(pl.multiple_of(x * PART, PART), PART)
    acc = jnp.concatenate(
        [own[pl.ds(pl.multiple_of(q * MEM + x * PART, PART), PART), :] for q in range(2)], 0
    )
    mem = fm[:, pl.ds(2 * c, 2), mine, :]
    mem = jnp.concatenate(
        [mem[0].reshape(2 * PART, HC), mem[1].reshape(2 * PART, HC)], 1
    ).astype(F32)
    for d in range(NX - 1):
        acc += rs[d].astype(F32)
    summed = mem + acc
    scaled = summed * lax.rsqrt(jnp.mean(summed * summed, axis=-1, keepdims=True) + 1e-06)
    st[c] = (scaled * gain_ref[...]).astype(BF)
    send(st.at[c], st.at[c], st_s, st_r, g, oc)
    arrived(st.at[oc], st_r, st_s)
    settled = st[...].reshape(MEM, D)
    mk[...] = nn(settled, wk[...]).astype(BF)
    mv[...] = nn(settled, wv[...]).astype(BF)

    loads[4].wait()
    def out_part(cc, h):
        return nn(mx[cc, h], wo[pl.ds(pl.multiple_of(cc * HC + h * HS, HS), HS), :])

    for h in range(HEADS):
        cols = slice(h * HS, (h + 1) * HS)
        q = qs[:, :, cols].reshape(2 * HALF, HS)
        scores = nt(q, mk[:, cols])
        high = jnp.max(scores, axis=1, keepdims=True)
        e = jnp.exp2((scores - high) * (SCALE * LOG2E))
        probs = (e / jnp.sum(e, axis=1, keepdims=True)).astype(BF)
        cross = nn(probs, mv[:, cols])
        both = lo[:, :, cols].reshape(2 * HALF, HS) + cross
        mx[c, h] = both.astype(BF)
        send(mx.at[c, h], mx.at[c, h], mx_s.at[h], mx_r.at[h], g, oc)
    acc = out_part(c, 0)
    for h in range(1, HEADS):
        acc += out_part(c, h)
    for h in range(HEADS):
        arrived(mx.at[oc, h], mx_r.at[h], mx_s.at[h])
        acc += out_part(oc, h)
    out_ref[...] = acc.astype(BF)

    for cp in sends:
        cp.wait_send()
    for k in range(1, TAILS):
        pl.when(row_start)(relayed[k].wait_send)


def shards(tokens, w_query, w_key, w_value, w_out, slot_query, span_decay, ffn_up, ffn_down, norm_gain):
    V = pltpu.VMEM
    DMA = pltpu.SemaphoreType.DMA
    scratch = [
        V((2, HALF, D), BF), V((2, HALF, D), BF),
        V((D, HC), BF), V((D, HC), BF), V((D, HC), BF), V((D, HC), BF),
        V((2, HALF, HC), BF), V((2, HALF, HC), BF), V((2, HALF, HC), BF),
        V((2, HALF, HC), BF), V((2, HALF, HC), BF),
        V((NZ, NY, 2, NX, 8, FS), BF),
        V((NX, ROWS, HS), BF), V((2, 8, 128), F32), V((2, 128, 128), F32),
        V((NX, ROWS, HS), BF), V((NX, 8, 128), F32),
        V((NY, ROWS, HS), BF), V((NY, 8, 128), F32),
        V((NZ, ROWS, HS), BF), V((NZ, 8, 128), F32),
        V((2, NX, NX * PART, HC), BF),
        V((NX, 2 * PART, D), BF), V((NX - 1, 2 * PART, D), BF), V((2 * MEM, D), F32),
        V((2 * MEM, D), BF), V((2 * MEM, D), BF), V((2, 2 * MEM, FS), BF),
        V((2, 2 * PART, D), BF),
        V((2, HALF, HC), F32),
        V((MEM, HC), BF), V((MEM, HC), BF),
        V((2, HEADS, 2 * HALF, HS), BF),
        V((128, 128), F32), V((TAILS, HALF // TAILS, D), BF),
        DMA((5,)), DMA((2,)), DMA((2,)), DMA((2,)), DMA((TAILS,)), DMA((TAILS,)), DMA((TAILS,)), DMA((TAILS,)),
        DMA((2, NX - 1)), DMA((2, NX - 1)), DMA((2, NZ // 2)), DMA((2, NZ // 2)),
        DMA((2, NZ)), DMA((2, NZ)), DMA((NZ,)), DMA((NZ,)),
        DMA((2, NX - 1)), DMA((2, NX - 1)), DMA((2, NY - 1)), DMA((2, NY - 1)),
        DMA((2, NZ - 1)), DMA((2, NZ - 1)),
        DMA((2, NX)), DMA((2, NX)), DMA((NX,)), DMA((NX,)), DMA, DMA, DMA((HEADS,)), DMA((HEADS,)),
    ]
    args = (
        tokens, w_query, w_key, w_value, w_out, slot_query, span_decay, ffn_up,
        ffn_down.T, norm_gain.reshape(1, D),
    )
    hbm = pl.BlockSpec(memory_space=pltpu.HBM)
    vm = pl.BlockSpec(memory_space=pltpu.VMEM)
    return pl.pallas_call(
        body,
        out_shape=jax.ShapeDtypeStruct((2 * HALF, HC), BF),
        in_specs=[hbm, hbm, hbm, hbm, hbm, vm, vm, hbm, hbm, vm],
        out_specs=vm,
        scratch_shapes=scratch,
        compiler_params=pltpu.CompilerParams(
            collective_id=0, has_side_effects=True, vmem_limit_bytes=48 * 1024 * 1024
        ),
    )(*[pltpu.with_memory_space_constraint(a, pltpu.HBM) for a in args])


def solution(mesh):
    in_specs = (
        P(("group", "seq"), None),
        P(None, "seq"),
        P(None, "seq"),
        P(None, "seq"),
        P(None, "seq"),
        P(None, "seq"),
        P("group", "seq"),
        P("group", "seq"),
        P("seq", "group"),
        P(),
    )
    out_specs = P("group", "seq")
    return jax.shard_map(shards, mesh=mesh, in_specs=in_specs, out_specs=out_specs, check_vma=False)
```

```python
import jax
import jax.numpy as jnp
from jax import lax
from jax.experimental import pallas as pl
from jax.experimental.pallas import tpu as pltpu
from jax.sharding import PartitionSpec as P

HS = 128
MEM = 64
NX, NY, NZ = 4, 4, 8
NG = NX * NY * NZ
HALF = 256
HC = 512
HEADS = 4
D = 1024
PART = MEM // NX
ROWS = HEADS * PART
FS = 512
TAILS = 4
FORWARD = (1, 3, 2)
MESH = pl.DeviceIdType.MESH
F32 = jnp.float32
BF = jnp.bfloat16
FLOOR = -1e30
NULL = 8.0
SCALE = HS ** (-0.5)
LOG2E = 1.4426950408889634


def nn(a, b):
    return lax.dot_general(a, b, (((1,), (0,)), ((), ())), preferred_element_type=F32)


def nt(a, b):
    return lax.dot_general(a, b, (((1,), (1,)), ((), ())), preferred_element_type=F32)


def stat_columns(peak, mass, rate, rows):
    lane = lax.broadcasted_iota(jnp.int32, (rows, 128), 1)
    return jnp.where(lane == 0, peak, jnp.where(lane == 1, mass, jnp.where(lane == 2, rate, 0.0)))


def before_item(items, stop):
    rate = jnp.zeros_like(items[0][0])
    shifted = [None] * len(items)
    for k in reversed(range(len(items))):
        live = k < stop
        shifted[k] = jnp.where(live, items[k][0] - rate, FLOOR)
        rate = rate + jnp.where(live, items[k][2], 0.0)
    peak = shifted[0]
    for a in shifted[1:]:
        peak = jnp.maximum(peak, a)
    weights = [jnp.where(k < stop, jnp.exp(a - peak), 0.0) for k, a in enumerate(shifted)]
    mass = jnp.zeros_like(rate)
    for w, item in zip(weights, items):
        mass = mass + item[1] * w
    return (peak, mass, rate), weights


def weighted(cols, first, values):
    total = cols[:, first : first + 1] * values[0].astype(F32)
    for k in range(1, len(values)):
        total = total + cols[:, first + k : first + k + 1] * values[k].astype(F32)
    return total


def body(
    tok_h, wq_h, wk_h, wv_h, wo_h, slot_h, decay_h, up_h, dn_h, gain_h, out_ref,
    tok, ptok, wq, wk, wv, wo, slot_ref, decay_ref, gain_ref, qs, ks, vs, kp, vp, ff,
    ps, pst, sc, xr, xst, yr, yst, zr, zst, fm, pb, rs, own, pc, pc_in, hid, st, lo, mk, mv, mx,
    tr, relay, load_sem, loc_sem, tok_s, tok_r, tail_s, tail_r, relay_s, relay_r, wx_s, wx_r, rg_s, rg_r, ny_s, ny_r, fy_s, fy_r,
    x_s, x_r, y_s, y_r, z_s, z_r, fm_s, fm_r, rs_s, rs_r, st_s, st_r, mx_s, mx_r,
):
    g = lax.axis_index("group")
    c = lax.axis_index("seq")
    x = lax.rem(g, NX)
    y = lax.rem(g // NX, NY)
    z = g // (NX * NY)
    oc = 1 - c

    def gid(zz, yy, xx):
        return zz * (NX * NY) + yy * NX + xx

    def xp(d):
        return lax.rem(x + d, NX)

    def yp(d):
        return lax.rem(y + d, NY)

    def zp(d):
        return lax.rem(z + d, NZ)

    nxt = lax.rem(g + 1, NG)
    prv = lax.rem(g + NG - 1, NG)
    down_row, up_row = lax.rem(g + NX, NG), lax.rem(g + NG - NX, NG)
    sends = []

    def send(src, dst, ss, rsem, gg, cc):
        cp = pltpu.make_async_remote_copy(
            src_ref=src, dst_ref=dst, send_sem=ss, recv_sem=rsem,
            device_id={"group": gg, "seq": cc}, device_id_type=MESH,
        )
        cp.start()
        sends.append(cp)
        return cp

    def arrived(ref, sem, ss):
        pltpu.make_async_remote_copy(
            src_ref=ref, dst_ref=ref, send_sem=ss, recv_sem=sem,
            device_id={"group": g, "seq": oc}, device_id_type=MESH,
        ).wait_recv()

    tr[...] = jnp.zeros_like(tr)
    barrier = pltpu.get_barrier_semaphore()

    def greet(gg, cc):
        pl.semaphore_signal(barrier, inc=1, device_id={"group": gg, "seq": cc}, device_id_type=MESH)

    greet(g, oc)
    for d in range(1, NX):
        greet(gid(z, y, xp(d)), c)
        greet(gid(z, y, xp(d)), oc)
    for d in range(1, NY):
        greet(gid(z, yp(d), x), c)
    for d in range(1, NZ):
        greet(gid(zp(d), y, x), c)
    greet(nxt, c)
    greet(prv, c)
    greet(down_row, c)
    greet(up_row, c)

    loads = []
    for k, (src, dst) in enumerate(
        (
            (tok_h, tok.at[c]), (wk_h, wk), (wv_h, wv), (wq_h, wq), (wo_h, wo),
            (slot_h, slot_ref), (decay_h, decay_ref), (gain_h, gain_ref),
        )
    ):
        cp = pltpu.make_async_copy(src, dst, load_sem.at[k])
        cp.start()
        loads.append(cp)
    lanes_x = pl.ds(pl.multiple_of(x * FS, FS), FS)
    wl = []
    for k, (src, dst) in enumerate(((up_h, ff), (dn_h, ff))):
        cp = pltpu.make_async_copy(src.at[:, lanes_x], dst.at[z, y, k, x], loc_sem.at[k])
        cp.start()
        wl.append(cp)

    def project(half):
        rows = tok[half]
        ks[half] = nn(rows, wk[...]).astype(BF)
        vs[half] = nn(rows, wv[...]).astype(BF)

    pl.semaphore_wait(barrier, 2 * (NX - 1) + (NY - 1) + (NZ - 1) + 5)

    send(tok_h, tok.at[c], tok_s.at[0], tok_r.at[0], g, oc)
    for k, (src, dst) in enumerate(((up_h, ff), (dn_h, ff))):
        for d in range(1, NX):
            to = xp(d)
            send(
                src.at[:, pl.ds(pl.multiple_of(to * FS, FS), FS)], dst.at[z, y, k, x],
                wx_s.at[k, d - 1], wx_r.at[k, d - 1], gid(z, y, to), c,
            )

    row_end = (x == NX - 1) & (g < NG - 1)
    row_start = (x == 0) & (g < NG - NX)
    follows = g > 0
    tails, handed, relayed = [], [], []
    for k in range(TAILS):
        rows = slice(k * (HALF // TAILS), (k + 1) * (HALF // TAILS))

        def piece(src, dst, ss, rsem, to):
            return pltpu.make_async_remote_copy(
                src_ref=src, dst_ref=dst, send_sem=ss, recv_sem=rsem,
                device_id={"group": to, "seq": c}, device_id_type=MESH,
            )

        there = ptok.at[c, rows]
        tails.append(piece(tok_h.at[rows], there, tail_s.at[k], tail_r.at[k], nxt))
        handed.append(
            piece(tok_h.at[rows], relay.at[k], tail_s.at[k], relay_r.at[k], gid(z, y, 0))
        )
        relayed.append(piece(relay.at[k], there, relay_s.at[k], tail_r.at[k], down_row))

    def tail_start(k, cond):
        pl.when(cond)(tails[k].start)

    def relay_start(k, cond):
        @pl.when(row_start & cond)
        def _():
            handed[k].wait_recv()
            relayed[k].start()

    tail_start(0, row_end)
    for cp in loads[:3]:
        cp.wait()
    project(c)

    left_y, right_y = yp(NY - 1), yp(1)
    left_z, right_z = zp(NZ - 1), zp(1)

    def weights_x():
        for k in range(2):
            wl[k].wait()
            for d in range(1, NX):
                arrived(ff.at[z, y, k, xp(NX - d)], wx_r.at[k, d - 1], wx_s.at[k, d - 1])

    def weights_ring(step):
        a, b = ff.at[zp(NZ + 1 - step), y], ff.at[zp(step - 1), y]
        if step == NZ // 2:
            a, b = a.at[0], b.at[1]
        send(a, a, rg_s.at[0, step - 1], rg_r.at[0, step - 1], gid(right_z, y, x), c)
        send(b, b, rg_s.at[1, step - 1], rg_r.at[1, step - 1], gid(left_z, y, x), c)

    def ring_wait(step):
        a, b = ff.at[zp(NZ - step), y], ff.at[zp(step), y]
        if step == NZ // 2:
            a, b = a.at[0], b.at[1]
        arrived(a, rg_r.at[0, step - 1], rg_s.at[0, step - 1])
        arrived(b, rg_r.at[1, step - 1], rg_s.at[1, step - 1])

    def weights_near(o):
        b = ff.at[zp(o), y]
        send(b, b, ny_s.at[0, o], ny_r.at[0, o], gid(z, right_y, x), c)
        send(b, b, ny_s.at[1, o], ny_r.at[1, o], gid(z, left_y, x), c)

    def weights_far(o):
        from_left = ff.at[zp(o), left_y]
        from_right = ff.at[zp(o), right_y]
        arrived(from_left, ny_r.at[0, o], ny_s.at[0, o])
        arrived(from_right, ny_r.at[1, o], ny_s.at[1, o])
        if o < NZ // 4:
            src, to = left_y, right_y
        elif o < NZ // 2:
            src = jnp.where(x == 0, right_y, left_y)
            to = jnp.where(x == 0, left_y, right_y)
        else:
            src, to = right_y, left_y
        b = ff.at[zp(o), src]
        send(b, b, fy_s.at[o], fy_r.at[o], gid(z, to, x), c)

    def weights_done():
        for o in range(NZ):
            arrived(ff.at[zp(o), yp(2)], fy_r.at[o], fy_s.at[o])

    arrived(tok.at[oc], tok_r.at[0], tok_s.at[0])
    project(oc)

    loads[5].wait()
    loads[6].wait()
    for h in range(HEADS):
        cols = slice(h * HS, (h + 1) * HS)
        keys = ks[:, :, cols].reshape(2 * HALF, HS)
        vals = vs[:, :, cols].reshape(2 * HALF, HS)
        scores = nt(slot_ref[:, cols], keys) * SCALE
        peak = jnp.max(scores, axis=1, keepdims=True)
        w = jnp.exp(scores - peak)
        mass = jnp.sum(w, axis=1, keepdims=True)
        pooled = nn(w.astype(BF), vals)
        stat = stat_columns(peak, mass, decay_ref[0:1, h : h + 1], MEM)
        for p in range(NX):
            rows = slice(p * PART, (p + 1) * PART)
            ps[p, h * PART : (h + 1) * PART, :] = pooled[rows].astype(BF)
            first = (p % 2) * ROWS + h * PART
            sc[p // 2, first : first + PART, :] = stat[rows]
    for q in range(2):
        pst[q] = jnp.transpose(sc[q])[0:8]

    for d in range(1, NX):
        to = xp(d)
        send(ps.at[to], xr.at[x], x_s.at[0, d - 1], x_r.at[0, d - 1], gid(z, y, to), c)
        send(pst.at[to // 2], xst.at[x], x_s.at[1, d - 1], x_r.at[1, d - 1], gid(z, y, to), c)
    for k in range(TAILS):
        tail_start(k, x < NX - 1)
        if k:
            pl.when(row_end)(handed[k].start)
    xr[x] = ps[x]
    xst[x] = pst[x // 2]
    weights_x()
    weights_ring(1)
    weights_near(0)
    loads[3].wait()
    for half in range(2):
        qs[half] = nn(tok[half], wq[...]).astype(BF)
    for d in range(1, NX):
        frm = xp(NX - d)
        arrived(xr.at[frm], x_r.at[0, d - 1], x_s.at[0, d - 1])
        arrived(xst.at[frm], x_r.at[1, d - 1], x_s.at[1, d - 1])
    odd = lax.rem(x, 2) == 1
    items = []
    for k in range(NX):
        tile = xst[k]
        tile = jnp.where(odd, pltpu.roll(tile, 64, 1), tile)
        items.append(tuple(tile[r : r + 1] for r in range(3)))
    in_row = [before_item(items, j) for j in range(NX + 1)]
    n = 0
    for j in range(1, NX + 1):
        for k in range(j):
            tr[n : n + 1] = in_row[j][1][k]
            n += 1
    cols = jnp.transpose(tr[...])[0:ROWS]
    row_val = [None]
    n = 0
    for j in range(1, NX + 1):
        row_val.append(weighted(cols, n, [xr[k] for k in range(j)]))
        n += j

    def stat_tile(state):
        sub = lax.broadcasted_iota(jnp.int32, (8, 128), 0)
        return jnp.where(sub == 0, state[0], jnp.where(sub == 1, state[1], state[2]))

    yr[y] = row_val[NX].astype(BF)
    yst[y] = stat_tile(in_row[NX][0])
    for d in range(1, NY):
        to = gid(z, yp(d), x)
        send(yr.at[y], yr.at[y], y_s.at[0, d - 1], y_r.at[0, d - 1], to, c)
        send(yst.at[y], yst.at[y], y_s.at[1, d - 1], y_r.at[1, d - 1], to, c)
    ring_wait(1)
    weights_ring(2)
    weights_near(1)
    weights_near(NZ - 1)
    for d in range(1, NY):
        frm = yp(NY - d)
        arrived(yr.at[frm], y_r.at[0, d - 1], y_s.at[0, d - 1])
        arrived(yst.at[frm], y_r.at[1, d - 1], y_s.at[1, d - 1])
    items = [tuple(yst[k, r : r + 1] for r in range(3)) for k in range(NY)]
    in_plane, w_some = before_item(items, y)
    plane, w_all = before_item(items, NY)
    for k in range(NY):
        tr[k : k + 1] = w_all[k]
        tr[NY + k : NY + k + 1] = w_some[k]
    cols = jnp.transpose(tr[...])[0:ROWS]
    vals = [yr[k] for k in range(NY)]

    zr[z] = weighted(cols, 0, vals).astype(BF)
    zst[z] = stat_tile(plane)
    for d in range(1, NZ):
        to = gid(zp(d), y, x)
        send(zr.at[z], zr.at[z], z_s.at[0, d - 1], z_r.at[0, d - 1], to, c)
        send(zst.at[z], zst.at[z], z_s.at[1, d - 1], z_r.at[1, d - 1], to, c)
    plane_val = weighted(cols, NY, vals)
    ring_wait(2)
    weights_ring(3)
    weights_near(2)
    weights_near(NZ - 2)
    weights_far(0)
    weights_far(1)
    weights_far(NZ - 1)
    relay_start(1, y < NY - 1)
    for d in range(1, NZ):
        frm = zp(NZ - d)
        arrived(zr.at[frm], z_r.at[0, d - 1], z_s.at[0, d - 1])
        arrived(zst.at[frm], z_r.at[1, d - 1], z_s.at[1, d - 1])
    items = [tuple(zst[k, r : r + 1] for r in range(3)) for k in range(NZ)]
    planes, w_some = before_item(items, z)
    for k in range(NZ):
        tr[k : k + 1] = w_some[k]
    n = NZ
    for j in range(NX):
        own_peak, own_mass, own_rate = in_row[j][0]
        shifted = [planes[0] - in_plane[2] - own_rate, in_plane[0] - own_rate, own_peak]
        peak = jnp.maximum(jnp.maximum(shifted[0], shifted[1]), shifted[2])
        parts = [jnp.exp(a - peak) for a in shifted]
        mass = planes[1] * parts[0] + in_plane[1] * parts[1] + own_mass * parts[2]
        anchor = jnp.maximum(peak, NULL)
        factor = jnp.exp(peak - anchor)
        coef = factor / (mass * factor + jnp.exp(NULL - anchor))
        for part in parts:
            tr[n : n + 1] = part * coef
            n += 1
    cols = jnp.transpose(tr[...])[0:ROWS]
    planes_val = weighted(cols, 0, [zr[k] for k in range(NZ)])
    for j in range(NX):
        vals = [planes_val, plane_val] + ([row_val[j]] if j else [])
        memory = weighted(cols, NZ + 3 * j, vals).astype(BF)
        for h in range(HEADS):
            fm[c, x, j * PART : (j + 1) * PART, h * HS : (h + 1) * HS] = memory[
                h * PART : (h + 1) * PART
            ]
    b = fm.at[c, x]
    for d in range(1, NX):
        send(b, b, fm_s.at[0, d], fm_r.at[0, d], gid(z, y, xp(d)), c)
    send(b, b, fm_s.at[1, 0], fm_r.at[1, 0], g, oc)
    weights_far(2)
    weights_far(NZ - 2)
    ring_wait(3)
    weights_ring(4)
    weights_near(3)
    weights_near(NZ - 3)
    relay_start(1, y == NY - 1)
    ring_wait(NZ // 2)
    weights_near(NZ // 2)
    quarter = HALF // 2
    parts = [slice(j * quarter, (j + 1) * quarter) for j in range(2)]
    across = [
        pltpu.make_async_remote_copy(
            src_ref=ptok.at[c, r], dst_ref=ptok.at[c, r], send_sem=tok_s.at[1 + j],
            recv_sem=tok_r.at[1 + j], device_id={"group": g, "seq": oc}, device_id_type=MESH,
        )
        for j, r in enumerate(parts)
    ]

    def project_prev(half, r):
        rows = ptok[half, r]
        kp[half, r] = nn(rows, wk[...]).astype(BF)
        vp[half, r] = nn(rows, wv[...]).astype(BF)

    def prev_take(j):
        for k in range(j * TAILS // 2, (j + 1) * TAILS // 2):
            tails[k].wait_recv()
        across[j].start()
        project_prev(c, parts[j])

    def prev_rest(j):
        arrived(ptok.at[oc, parts[j]], tok_r.at[1 + j], tok_s.at[1 + j])
        project_prev(oc, parts[j])

    for d in FORWARD:
        b = fm.at[c, xp(NX - d)]
        arrived(b, fm_r.at[0, d], fm_s.at[0, d])
        send(b, b, fm_s.at[1, d], fm_r.at[1, d], g, oc)
    pl.when(follows)(lambda: prev_take(0))
    weights_far(3)
    weights_far(NZ - 3)
    weights_far(NZ // 2)
    relay_start(2, True)
    relay_start(3, True)
    pl.when(follows)(lambda: prev_rest(0))
    arrived(fm.at[oc, x], fm_r.at[1, 0], fm_s.at[1, 0])
    for d in FORWARD:
        arrived(fm.at[oc, xp(NX - d)], fm_r.at[1, d], fm_s.at[1, d])
    weights_done()
    up = ff[:, :, 0].reshape(D, FS)
    total = nn(fm[0].reshape(NX * MEM, HC), up[0:HC]) + nn(fm[1].reshape(NX * MEM, HC), up[HC:])
    hid[...] = jax.nn.gelu(total, approximate=True).astype(BF).reshape(2, 2 * MEM, FS)
    down = ff[:, :, 1].reshape(D, FS)
    pc[...] = nt(hid[oc], down).astype(BF)
    send(pc, pc_in, rs_s.at[0], rs_r.at[0], g, oc)
    own[...] = nt(hid[c], down)
    arrived(pc_in, rs_r.at[0], rs_s.at[0])
    own[...] += pc_in[...].astype(F32)
    for j in range(NX):
        for q in range(2):
            first = q * MEM + j * PART
            pb[j, q * PART : (q + 1) * PART, :] = own[first : first + PART].astype(BF)
    for d in FORWARD:
        to = xp(d)
        send(pb.at[to], rs.at[d - 1], rs_s.at[d], rs_r.at[d], gid(z, y, to), c)
    @pl.when(follows)
    def _():
        prev_take(1)
        prev_rest(1)

    @pl.when(g == 0)
    def _():
        kp[...] = jnp.zeros_like(kp)
        vp[...] = jnp.zeros_like(vp)

    row_i = lax.broadcasted_iota(jnp.int32, (HALF, HALF), 0)
    col_i = lax.broadcasted_iota(jnp.int32, (HALF, HALF), 1)
    tri = col_i <= row_i
    bias = jnp.where(g == 0, FLOOR, 0.0).astype(F32)

    def attend(h, i):
        cols = slice(h * HS, (h + 1) * HS)
        q = qs[i, :, cols]
        near = nt(q, ks[i, :, cols])
        far = nt(q, kp[i, :, cols]) + bias
        diag = jnp.where(tri, near, far)
        if i == 0:
            full = nt(q, kp[1, :, cols]) + bias
            full_v = vp[1, :, cols]
        else:
            full = nt(q, ks[0, :, cols])
            full_v = vs[0, :, cols]
        high = jnp.maximum(
            jnp.max(diag, axis=1, keepdims=True), jnp.max(full, axis=1, keepdims=True)
        )
        ed = jnp.exp2((diag - high) * (SCALE * LOG2E))
        ef = jnp.exp2((full - high) * (SCALE * LOG2E))
        mass = jnp.sum(ed, axis=1, keepdims=True) + jnp.sum(ef, axis=1, keepdims=True)
        acc = nn(jnp.where(tri, ed, 0.0).astype(BF), vs[i, :, cols])
        acc += nn(jnp.where(tri, 0.0, ed).astype(BF), vp[i, :, cols])
        acc += nn(ef.astype(BF), full_v)
        lo[i, :, cols] = acc / mass

    for h in range(HEADS):
        for i in range(2):
            attend(h, i)
    loads[4].wait()
    loads[7].wait()
    for d in FORWARD:
        arrived(rs.at[d - 1], rs_r.at[d], rs_s.at[d])
    mine = pl.ds(pl.multiple_of(x * PART, PART), PART)
    acc = jnp.concatenate(
        [own[pl.ds(pl.multiple_of(q * MEM + x * PART, PART), PART), :] for q in range(2)], 0
    )
    mem = fm[:, pl.ds(2 * c, 2), mine, :]
    mem = jnp.concatenate(
        [mem[0].reshape(2 * PART, HC), mem[1].reshape(2 * PART, HC)], 1
    ).astype(F32)
    for d in range(NX - 1):
        acc += rs[d].astype(F32)
    summed = mem + acc
    scaled = summed * lax.rsqrt(jnp.mean(summed * summed, axis=-1, keepdims=True) + 1e-06)
    st[c] = (scaled * gain_ref[...]).astype(BF)
    send(st.at[c], st.at[c], st_s, st_r, g, oc)
    arrived(st.at[oc], st_r, st_s)
    settled = st[...].reshape(MEM, D)
    mk[...] = nn(settled, wk[...]).astype(BF)
    mv[...] = nn(settled, wv[...]).astype(BF)

    def out_part(cc, h):
        return nn(mx[cc, h], wo[pl.ds(pl.multiple_of(cc * HC + h * HS, HS), HS), :])

    for h in range(HEADS):
        cols = slice(h * HS, (h + 1) * HS)
        q = qs[:, :, cols].reshape(2 * HALF, HS)
        scores = nt(q, mk[:, cols])
        high = jnp.max(scores, axis=1, keepdims=True)
        e = jnp.exp2((scores - high) * (SCALE * LOG2E))
        probs = (e / jnp.sum(e, axis=1, keepdims=True)).astype(BF)
        cross = nn(probs, mv[:, cols])
        both = lo[:, :, cols].reshape(2 * HALF, HS) + cross
        mx[c, h] = both.astype(BF)
        send(mx.at[c, h], mx.at[c, h], mx_s.at[h], mx_r.at[h], g, oc)
    acc = out_part(c, 0)
    for h in range(1, HEADS):
        acc += out_part(c, h)
    for h in range(HEADS):
        arrived(mx.at[oc, h], mx_r.at[h], mx_s.at[h])
        acc += out_part(oc, h)
    out_ref[...] = acc.astype(BF)

    for cp in sends:
        cp.wait_send()
    for k in range(TAILS):
        pl.when(g < NG - 1)(tails[k].wait_send)
        if k:
            pl.when(row_start)(relayed[k].wait_send)
    for cp in across:
        pl.when(follows)(cp.wait_send)


def shards(tokens, w_query, w_key, w_value, w_out, slot_query, span_decay, ffn_up, ffn_down, norm_gain):
    V = pltpu.VMEM
    DMA = pltpu.SemaphoreType.DMA
    scratch = [
        V((2, HALF, D), BF), V((2, HALF, D), BF),
        V((D, HC), BF), V((D, HC), BF), V((D, HC), BF), V((D, HC), BF),
        V((MEM, HC), BF), V((1, HEADS), F32), V((1, D), F32),
        V((2, HALF, HC), BF), V((2, HALF, HC), BF), V((2, HALF, HC), BF),
        V((2, HALF, HC), BF), V((2, HALF, HC), BF),
        V((NZ, NY, 2, NX, 8, FS), BF),
        V((NX, ROWS, HS), BF), V((2, 8, 128), F32), V((2, 128, 128), F32),
        V((NX, ROWS, HS), BF), V((NX, 8, 128), F32),
        V((NY, ROWS, HS), BF), V((NY, 8, 128), F32),
        V((NZ, ROWS, HS), BF), V((NZ, 8, 128), F32),
        V((2, NX, NX * PART, HC), BF),
        V((NX, 2 * PART, D), BF), V((NX - 1, 2 * PART, D), BF), V((2 * MEM, D), F32),
        V((2 * MEM, D), BF), V((2 * MEM, D), BF), V((2, 2 * MEM, FS), BF),
        V((2, 2 * PART, D), BF),
        V((2, HALF, HC), F32),
        V((MEM, HC), BF), V((MEM, HC), BF),
        V((2, HEADS, 2 * HALF, HS), BF),
        V((128, 128), F32), V((TAILS, HALF // TAILS, D), BF),
        DMA((8,)), DMA((2,)), DMA((3,)), DMA((3,)), DMA((TAILS,)), DMA((TAILS,)), DMA((TAILS,)), DMA((TAILS,)),
        DMA((2, NX - 1)), DMA((2, NX - 1)), DMA((2, NZ // 2)), DMA((2, NZ // 2)),
        DMA((2, NZ)), DMA((2, NZ)), DMA((NZ,)), DMA((NZ,)),
        DMA((2, NX - 1)), DMA((2, NX - 1)), DMA((2, NY - 1)), DMA((2, NY - 1)),
        DMA((2, NZ - 1)), DMA((2, NZ - 1)),
        DMA((2, NX)), DMA((2, NX)), DMA((NX,)), DMA((NX,)), DMA, DMA, DMA((HEADS,)), DMA((HEADS,)),
    ]
    args = (
        tokens, w_query, w_key, w_value, w_out, slot_query, span_decay, ffn_up,
        ffn_down.T, norm_gain.reshape(1, D),
    )
    hbm = pl.BlockSpec(memory_space=pltpu.HBM)
    vm = pl.BlockSpec(memory_space=pltpu.VMEM)
    return pl.pallas_call(
        body,
        out_shape=jax.ShapeDtypeStruct((2 * HALF, HC), BF),
        in_specs=[hbm] * 10,
        out_specs=vm,
        scratch_shapes=scratch,
        compiler_params=pltpu.CompilerParams(
            collective_id=0, has_side_effects=True, vmem_limit_bytes=48 * 1024 * 1024
        ),
    )(*[pltpu.with_memory_space_constraint(a, pltpu.HBM) for a in args])


def solution(mesh):
    in_specs = (
        P(("group", "seq"), None),
        P(None, "seq"),
        P(None, "seq"),
        P(None, "seq"),
        P(None, "seq"),
        P(None, "seq"),
        P("group", "seq"),
        P("group", "seq"),
        P("seq", "group"),
        P(),
    )
    out_specs = P("group", "seq")
    return jax.shard_map(shards, mesh=mesh, in_specs=in_specs, out_specs=out_specs, check_vma=False)
```

```python
import jax
import jax.numpy as jnp
from jax import lax
from jax.experimental import pallas as pl
from jax.experimental.pallas import tpu as pltpu
from jax.sharding import PartitionSpec as P

HS = 128
MEM = 64
NX, NY, NZ = 4, 4, 8
NG = NX * NY * NZ
HALF = 256
HC = 512
HEADS = 4
D = 1024
PART = MEM // NX
ROWS = HEADS * PART
FS = 512
TAILS = 4
FORWARD = (1, 3, 2)
MESH = pl.DeviceIdType.MESH
F32 = jnp.float32
BF = jnp.bfloat16
FLOOR = -1e30
NULL = 8.0
SCALE = HS ** (-0.5)
LOG2E = 1.4426950408889634


def nn(a, b):
    return lax.dot_general(a, b, (((1,), (0,)), ((), ())), preferred_element_type=F32)


def nt(a, b):
    return lax.dot_general(a, b, (((1,), (1,)), ((), ())), preferred_element_type=F32)


def stat_columns(peak, mass, rate, rows):
    lane = lax.broadcasted_iota(jnp.int32, (rows, 128), 1)
    return jnp.where(lane == 0, peak, jnp.where(lane == 1, mass, jnp.where(lane == 2, rate, 0.0)))


def before_item(items, stop):
    rate = jnp.zeros_like(items[0][0])
    shifted = [None] * len(items)
    for k in reversed(range(len(items))):
        live = k < stop
        shifted[k] = jnp.where(live, items[k][0] - rate, FLOOR)
        rate = rate + jnp.where(live, items[k][2], 0.0)
    peak = shifted[0]
    for a in shifted[1:]:
        peak = jnp.maximum(peak, a)
    weights = [jnp.where(k < stop, jnp.exp(a - peak), 0.0) for k, a in enumerate(shifted)]
    mass = jnp.zeros_like(rate)
    for w, item in zip(weights, items):
        mass = mass + item[1] * w
    return (peak, mass, rate), weights


def weighted(cols, first, values):
    total = cols[:, first : first + 1] * values[0].astype(F32)
    for k in range(1, len(values)):
        total = total + cols[:, first + k : first + k + 1] * values[k].astype(F32)
    return total


def body(
    tok_h, wq_h, wk_h, wv_h, wo_h, slot_h, decay_h, up_h, dn_h, gain_h, out_ref,
    tok, ptok, wq, wk, wv, wo, slot_ref, decay_ref, gain_ref, qs, ks, vs, kp, vp, ff,
    ps, pst, sc, xr, xst, yr, yst, zr, zst, fm, pb, rs, own, pc, pc_in, hid, st, lo, mk, mv, mx,
    tr, relay, load_sem, loc_sem, tok_s, tok_r, tail_s, tail_r, relay_s, relay_r, wx_s, wx_r, rg_s, rg_r, ny_s, ny_r, fy_s, fy_r,
    x_s, x_r, y_s, y_r, z_s, z_r, fm_s, fm_r, pc_s, pc_r, rs_s, rs_r, st_s, st_r, mx_s, mx_r,
):
    g = lax.axis_index("group")
    c = lax.axis_index("seq")
    x = lax.rem(g, NX)
    y = lax.rem(g // NX, NY)
    z = g // (NX * NY)
    oc = 1 - c

    def gid(zz, yy, xx):
        return zz * (NX * NY) + yy * NX + xx

    def xp(d):
        return lax.rem(x + d, NX)

    def yp(d):
        return lax.rem(y + d, NY)

    def zp(d):
        return lax.rem(z + d, NZ)

    nxt = lax.rem(g + 1, NG)
    prv = lax.rem(g + NG - 1, NG)
    down_row, up_row = lax.rem(g + NX, NG), lax.rem(g + NG - NX, NG)
    sends = []

    def send(src, dst, ss, rsem, gg, cc):
        cp = pltpu.make_async_remote_copy(
            src_ref=src, dst_ref=dst, send_sem=ss, recv_sem=rsem,
            device_id={"group": gg, "seq": cc}, device_id_type=MESH,
        )
        cp.start()
        sends.append(cp)
        return cp

    def arrived(ref, sem, ss):
        pltpu.make_async_remote_copy(
            src_ref=ref, dst_ref=ref, send_sem=ss, recv_sem=sem,
            device_id={"group": g, "seq": oc}, device_id_type=MESH,
        ).wait_recv()

    tr[...] = jnp.zeros_like(tr)
    barrier = pltpu.get_barrier_semaphore()

    def greet(gg, cc):
        pl.semaphore_signal(barrier, inc=1, device_id={"group": gg, "seq": cc}, device_id_type=MESH)

    greet(g, oc)
    for d in range(1, NX):
        greet(gid(z, y, xp(d)), c)
        greet(gid(z, y, xp(d)), oc)
    for d in range(1, NY):
        greet(gid(z, yp(d), x), c)
    for d in range(1, NZ):
        greet(gid(zp(d), y, x), c)
    greet(nxt, c)
    greet(prv, c)
    greet(down_row, c)
    greet(up_row, c)

    loads = []
    for k, (src, dst) in enumerate(
        (
            (tok_h, tok.at[c]), (wk_h, wk), (wv_h, wv), (wq_h, wq), (wo_h, wo),
            (slot_h, slot_ref), (decay_h, decay_ref), (gain_h, gain_ref),
        )
    ):
        cp = pltpu.make_async_copy(src, dst, load_sem.at[k])
        cp.start()
        loads.append(cp)
    lanes_x = pl.ds(pl.multiple_of(x * FS, FS), FS)
    wl = []
    for k, (src, dst) in enumerate(((up_h, ff), (dn_h, ff))):
        cp = pltpu.make_async_copy(src.at[:, lanes_x], dst.at[z, y, k, x], loc_sem.at[k])
        cp.start()
        wl.append(cp)

    def project(half):
        rows = tok[half]
        ks[half] = nn(rows, wk[...]).astype(BF)
        vs[half] = nn(rows, wv[...]).astype(BF)

    pl.semaphore_wait(barrier, 2 * (NX - 1) + (NY - 1) + (NZ - 1) + 5)

    send(tok_h, tok.at[c], tok_s.at[0], tok_r.at[0], g, oc)
    for k, (src, dst) in enumerate(((up_h, ff), (dn_h, ff))):
        for d in range(1, NX):
            to = xp(d)
            send(
                src.at[:, pl.ds(pl.multiple_of(to * FS, FS), FS)], dst.at[z, y, k, x],
                wx_s.at[k, d - 1], wx_r.at[k, d - 1], gid(z, y, to), c,
            )

    row_end = (x == NX - 1) & (g < NG - 1)
    row_start = (x == 0) & (g < NG - NX)
    follows = g > 0
    tails, handed, relayed = [], [], []
    for k in range(TAILS):
        rows = slice(k * (HALF // TAILS), (k + 1) * (HALF // TAILS))

        def piece(src, dst, ss, rsem, to):
            return pltpu.make_async_remote_copy(
                src_ref=src, dst_ref=dst, send_sem=ss, recv_sem=rsem,
                device_id={"group": to, "seq": c}, device_id_type=MESH,
            )

        there = ptok.at[c, rows]
        tails.append(piece(tok_h.at[rows], there, tail_s.at[k], tail_r.at[k], nxt))
        handed.append(
            piece(tok_h.at[rows], relay.at[k], tail_s.at[k], relay_r.at[k], gid(z, y, 0))
        )
        relayed.append(piece(relay.at[k], there, relay_s.at[k], tail_r.at[k], down_row))

    def tail_start(k, cond):
        pl.when(cond)(tails[k].start)

    def relay_start(k, cond):
        @pl.when(row_start & cond)
        def _():
            handed[k].wait_recv()
            relayed[k].start()

    tail_start(0, row_end)
    for cp in loads[:3]:
        cp.wait()
    project(c)

    left_y, right_y = yp(NY - 1), yp(1)
    left_z, right_z = zp(NZ - 1), zp(1)

    def weights_x():
        for k in range(2):
            wl[k].wait()
            for d in range(1, NX):
                arrived(ff.at[z, y, k, xp(NX - d)], wx_r.at[k, d - 1], wx_s.at[k, d - 1])

    def weights_ring(step, row=y, lane=0):
        a, b = ff.at[zp(NZ + 1 - step), row], ff.at[zp(step - 1), row]
        if step == NZ // 2:
            a, b = a.at[0], b.at[1]
        k = step - 1
        send(a, a, rg_s.at[lane, 0, k], rg_r.at[lane, 0, k], gid(right_z, y, x), c)
        send(b, b, rg_s.at[lane, 1, k], rg_r.at[lane, 1, k], gid(left_z, y, x), c)

    def ring_wait(step, row=y, lane=0):
        a, b = ff.at[zp(NZ - step), row], ff.at[zp(step), row]
        if step == NZ // 2:
            a, b = a.at[0], b.at[1]
        arrived(a, rg_r.at[lane, 0, step - 1], rg_s.at[lane, 0, step - 1])
        arrived(b, rg_r.at[lane, 1, step - 1], rg_s.at[lane, 1, step - 1])

    far_y = yp(2)

    def far_ring(step):
        if step == 1:
            arrived(ff.at[z, far_y], fy_r, fy_s)
        else:
            ring_wait(step - 1, far_y, 1)
        weights_ring(step, far_y, 1)

    def weights_near(o):
        b = ff.at[zp(o), y]
        send(b, b, ny_s.at[0, o], ny_r.at[0, o], gid(z, right_y, x), c)
        send(b, b, ny_s.at[1, o], ny_r.at[1, o], gid(z, left_y, x), c)

    def near_wait(o):
        arrived(ff.at[zp(o), left_y], ny_r.at[0, o], ny_s.at[0, o])
        arrived(ff.at[zp(o), right_y], ny_r.at[1, o], ny_s.at[1, o])

    def weights_far():
        near_wait(0)
        b = ff.at[z, left_y]
        send(b, b, fy_s, fy_r, gid(z, right_y, x), c)

    def weights_done():
        for o in range(1, NZ):
            near_wait(o)
        ring_wait(NZ // 2, far_y, 1)

    arrived(tok.at[oc], tok_r.at[0], tok_s.at[0])
    project(oc)

    loads[5].wait()
    loads[6].wait()
    for h in range(HEADS):
        cols = slice(h * HS, (h + 1) * HS)
        keys = ks[:, :, cols].reshape(2 * HALF, HS)
        vals = vs[:, :, cols].reshape(2 * HALF, HS)
        scores = nt(slot_ref[:, cols], keys) * SCALE
        peak = jnp.max(scores, axis=1, keepdims=True)
        w = jnp.exp(scores - peak)
        mass = jnp.sum(w, axis=1, keepdims=True)
        pooled = nn(w.astype(BF), vals)
        stat = stat_columns(peak, mass, decay_ref[0:1, h : h + 1], MEM)
        for p in range(NX):
            rows = slice(p * PART, (p + 1) * PART)
            ps[p, h * PART : (h + 1) * PART, :] = pooled[rows].astype(BF)
            first = (p % 2) * ROWS + h * PART
            sc[p // 2, first : first + PART, :] = stat[rows]
    for q in range(2):
        pst[q] = jnp.transpose(sc[q])[0:8]

    for d in range(1, NX):
        to = xp(d)
        send(ps.at[to], xr.at[x], x_s.at[0, d - 1], x_r.at[0, d - 1], gid(z, y, to), c)
        send(pst.at[to // 2], xst.at[x], x_s.at[1, d - 1], x_r.at[1, d - 1], gid(z, y, to), c)
    for k in range(TAILS):
        tail_start(k, x < NX - 1)
        if k:
            pl.when(row_end)(handed[k].start)
    xr[x] = ps[x]
    xst[x] = pst[x // 2]
    weights_x()
    weights_ring(1)
    weights_near(0)
    loads[3].wait()
    for half in range(2):
        qs[half] = nn(tok[half], wq[...]).astype(BF)
    for d in range(1, NX):
        frm = xp(NX - d)
        arrived(xr.at[frm], x_r.at[0, d - 1], x_s.at[0, d - 1])
        arrived(xst.at[frm], x_r.at[1, d - 1], x_s.at[1, d - 1])
    odd = lax.rem(x, 2) == 1
    items = []
    for k in range(NX):
        tile = xst[k]
        tile = jnp.where(odd, pltpu.roll(tile, 64, 1), tile)
        items.append(tuple(tile[r : r + 1] for r in range(3)))
    in_row = [before_item(items, j) for j in range(NX + 1)]
    n = 0
    for j in range(1, NX + 1):
        for k in range(j):
            tr[n : n + 1] = in_row[j][1][k]
            n += 1
    cols = jnp.transpose(tr[...])[0:ROWS]
    row_val = [None]
    n = 0
    for j in range(1, NX + 1):
        row_val.append(weighted(cols, n, [xr[k] for k in range(j)]))
        n += j

    def stat_tile(state):
        sub = lax.broadcasted_iota(jnp.int32, (8, 128), 0)
        return jnp.where(sub == 0, state[0], jnp.where(sub == 1, state[1], state[2]))

    yr[y] = row_val[NX].astype(BF)
    yst[y] = stat_tile(in_row[NX][0])
    for d in range(1, NY):
        to = gid(z, yp(d), x)
        send(yr.at[y], yr.at[y], y_s.at[0, d - 1], y_r.at[0, d - 1], to, c)
        send(yst.at[y], yst.at[y], y_s.at[1, d - 1], y_r.at[1, d - 1], to, c)
    ring_wait(1)
    weights_ring(2)
    weights_far()
    weights_near(1)
    weights_near(NZ - 1)
    for d in range(1, NY):
        frm = yp(NY - d)
        arrived(yr.at[frm], y_r.at[0, d - 1], y_s.at[0, d - 1])
        arrived(yst.at[frm], y_r.at[1, d - 1], y_s.at[1, d - 1])
    items = [tuple(yst[k, r : r + 1] for r in range(3)) for k in range(NY)]
    in_plane, w_some = before_item(items, y)
    plane, w_all = before_item(items, NY)
    for k in range(NY):
        tr[k : k + 1] = w_all[k]
        tr[NY + k : NY + k + 1] = w_some[k]
    cols = jnp.transpose(tr[...])[0:ROWS]
    vals = [yr[k] for k in range(NY)]

    zr[z] = weighted(cols, 0, vals).astype(BF)
    zst[z] = stat_tile(plane)
    for d in range(1, NZ):
        to = gid(zp(d), y, x)
        send(zr.at[z], zr.at[z], z_s.at[0, d - 1], z_r.at[0, d - 1], to, c)
        send(zst.at[z], zst.at[z], z_s.at[1, d - 1], z_r.at[1, d - 1], to, c)
    plane_val = weighted(cols, NY, vals)
    far_ring(1)
    ring_wait(2)
    weights_ring(3)
    weights_near(2)
    weights_near(NZ - 2)
    relay_start(1, y < NY - 1)
    for d in range(1, NZ):
        frm = zp(NZ - d)
        arrived(zr.at[frm], z_r.at[0, d - 1], z_s.at[0, d - 1])
        arrived(zst.at[frm], z_r.at[1, d - 1], z_s.at[1, d - 1])
    items = [tuple(zst[k, r : r + 1] for r in range(3)) for k in range(NZ)]
    planes, w_some = before_item(items, z)
    for k in range(NZ):
        tr[k : k + 1] = w_some[k]
    n = NZ
    for j in range(NX):
        own_peak, own_mass, own_rate = in_row[j][0]
        shifted = [planes[0] - in_plane[2] - own_rate, in_plane[0] - own_rate, own_peak]
        peak = jnp.maximum(jnp.maximum(shifted[0], shifted[1]), shifted[2])
        parts = [jnp.exp(a - peak) for a in shifted]
        mass = planes[1] * parts[0] + in_plane[1] * parts[1] + own_mass * parts[2]
        anchor = jnp.maximum(peak, NULL)
        factor = jnp.exp(peak - anchor)
        coef = factor / (mass * factor + jnp.exp(NULL - anchor))
        for part in parts:
            tr[n : n + 1] = part * coef
            n += 1
    cols = jnp.transpose(tr[...])[0:ROWS]
    planes_val = weighted(cols, 0, [zr[k] for k in range(NZ)])
    for j in range(NX):
        vals = [planes_val, plane_val] + ([row_val[j]] if j else [])
        memory = weighted(cols, NZ + 3 * j, vals).astype(BF)
        for h in range(HEADS):
            fm[c, x, j * PART : (j + 1) * PART, h * HS : (h + 1) * HS] = memory[
                h * PART : (h + 1) * PART
            ]
    b = fm.at[c, x]
    for d in range(1, NX):
        send(b, b, fm_s.at[0, d], fm_r.at[0, d], gid(z, y, xp(d)), c)
    send(b, b, fm_s.at[1, 0], fm_r.at[1, 0], g, oc)
    far_ring(2)
    ring_wait(3)
    weights_ring(4)
    weights_near(3)
    weights_near(NZ - 3)
    relay_start(1, y == NY - 1)
    ring_wait(NZ // 2)
    weights_near(NZ // 2)
    far_ring(3)
    quarter = HALF // 2
    parts = [slice(j * quarter, (j + 1) * quarter) for j in range(2)]
    across = [
        pltpu.make_async_remote_copy(
            src_ref=ptok.at[c, r], dst_ref=ptok.at[c, r], send_sem=tok_s.at[1 + j],
            recv_sem=tok_r.at[1 + j], device_id={"group": g, "seq": oc}, device_id_type=MESH,
        )
        for j, r in enumerate(parts)
    ]

    def project_prev(half, r):
        rows = ptok[half, r]
        kp[half, r] = nn(rows, wk[...]).astype(BF)
        vp[half, r] = nn(rows, wv[...]).astype(BF)

    def prev_take(j):
        for k in range(j * TAILS // 2, (j + 1) * TAILS // 2):
            tails[k].wait_recv()
        across[j].start()
        project_prev(c, parts[j])

    def prev_rest(j):
        arrived(ptok.at[oc, parts[j]], tok_r.at[1 + j], tok_s.at[1 + j])
        project_prev(oc, parts[j])

    for d in FORWARD:
        b = fm.at[c, xp(NX - d)]
        arrived(b, fm_r.at[0, d], fm_s.at[0, d])
        send(b, b, fm_s.at[1, d], fm_r.at[1, d], g, oc)
    pl.when(follows)(lambda: prev_take(0))
    far_ring(NZ // 2)
    relay_start(2, True)
    relay_start(3, True)
    pl.when(follows)(lambda: prev_rest(0))
    arrived(fm.at[oc, x], fm_r.at[1, 0], fm_s.at[1, 0])
    for d in FORWARD:
        arrived(fm.at[oc, xp(NX - d)], fm_r.at[1, d], fm_s.at[1, d])
    weights_done()
    up = ff[:, :, 0].reshape(D, FS)
    total = nn(fm[0].reshape(NX * MEM, HC), up[0:HC]) + nn(fm[1].reshape(NX * MEM, HC), up[HC:])
    hid[...] = jax.nn.gelu(total, approximate=True).astype(BF).reshape(2, 2 * MEM, FS)
    down = ff[:, :, 1].reshape(D, FS)
    for k in range(2):
        pc[k] = nt(hid[oc], down[k * HC : (k + 1) * HC]).astype(BF)
        send(pc.at[k], pc_in.at[k], pc_s.at[k], pc_r.at[k], g, oc)
    own[...] = nt(hid[c], down)
    for k in range(2):
        arrived(pc_in.at[k], pc_r.at[k], pc_s.at[k])
    own[...] += jnp.concatenate([pc_in[0], pc_in[1]], 1).astype(F32)
    for j in range(NX):
        for q in range(2):
            first = q * MEM + j * PART
            pb[j, q * PART : (q + 1) * PART, :] = own[first : first + PART].astype(BF)
    for d in FORWARD:
        to = xp(d)
        send(pb.at[to], rs.at[d - 1], rs_s.at[d], rs_r.at[d], gid(z, y, to), c)
    @pl.when(follows)
    def _():
        prev_take(1)
        prev_rest(1)

    @pl.when(g == 0)
    def _():
        kp[...] = jnp.zeros_like(kp)
        vp[...] = jnp.zeros_like(vp)

    row_i = lax.broadcasted_iota(jnp.int32, (HALF, HALF), 0)
    col_i = lax.broadcasted_iota(jnp.int32, (HALF, HALF), 1)
    tri = col_i <= row_i
    bias = jnp.where(g == 0, FLOOR, 0.0).astype(F32)

    def attend(h, i):
        cols = slice(h * HS, (h + 1) * HS)
        q = qs[i, :, cols]
        near = nt(q, ks[i, :, cols])
        far = nt(q, kp[i, :, cols]) + bias
        diag = jnp.where(tri, near, far)
        if i == 0:
            full = nt(q, kp[1, :, cols]) + bias
            full_v = vp[1, :, cols]
        else:
            full = nt(q, ks[0, :, cols])
            full_v = vs[0, :, cols]
        high = jnp.maximum(
            jnp.max(diag, axis=1, keepdims=True), jnp.max(full, axis=1, keepdims=True)
        )
        ed = jnp.exp2((diag - high) * (SCALE * LOG2E))
        ef = jnp.exp2((full - high) * (SCALE * LOG2E))
        mass = jnp.sum(ed, axis=1, keepdims=True) + jnp.sum(ef, axis=1, keepdims=True)
        acc = nn(jnp.where(tri, ed, 0.0).astype(BF), vs[i, :, cols])
        acc += nn(jnp.where(tri, 0.0, ed).astype(BF), vp[i, :, cols])
        acc += nn(ef.astype(BF), full_v)
        lo[i, :, cols] = acc / mass

    for h in range(HEADS):
        for i in range(2):
            attend(h, i)
    loads[4].wait()
    loads[7].wait()
    for d in FORWARD:
        arrived(rs.at[d - 1], rs_r.at[d], rs_s.at[d])
    mine = pl.ds(pl.multiple_of(x * PART, PART), PART)
    acc = jnp.concatenate(
        [own[pl.ds(pl.multiple_of(q * MEM + x * PART, PART), PART), :] for q in range(2)], 0
    )
    mem = fm[:, pl.ds(2 * c, 2), mine, :]
    mem = jnp.concatenate(
        [mem[0].reshape(2 * PART, HC), mem[1].reshape(2 * PART, HC)], 1
    ).astype(F32)
    for d in range(NX - 1):
        acc += rs[d].astype(F32)
    summed = mem + acc
    scaled = summed * lax.rsqrt(jnp.mean(summed * summed, axis=-1, keepdims=True) + 1e-06)
    st[c] = (scaled * gain_ref[...]).astype(BF)
    send(st.at[c], st.at[c], st_s, st_r, g, oc)
    arrived(st.at[oc], st_r, st_s)
    settled = st[...].reshape(MEM, D)
    mk[...] = nn(settled, wk[...]).astype(BF)
    mv[...] = nn(settled, wv[...]).astype(BF)

    def out_part(cc, h):
        return nn(mx[cc, h], wo[pl.ds(pl.multiple_of(cc * HC + h * HS, HS), HS), :])

    def cross_head(h):
        cols = slice(h * HS, (h + 1) * HS)
        q = qs[:, :, cols].reshape(2 * HALF, HS)
        scores = nt(q, mk[:, cols])
        high = jnp.max(scores, axis=1, keepdims=True)
        e = jnp.exp2((scores - high) * (SCALE * LOG2E))
        probs = (e / jnp.sum(e, axis=1, keepdims=True)).astype(BF)
        both = lo[:, :, cols].reshape(2 * HALF, HS) + nn(probs, mv[:, cols])
        return both.astype(BF)

    for h in range(0, HEADS, 2):
        pair = [cross_head(h), cross_head(h + 1)]
        for k in range(2):
            mx[c, h + k] = pair[k]
        for k in range(2):
            b = mx.at[c, h + k]
            send(b, b, mx_s.at[h + k], mx_r.at[h + k], g, oc)
    acc = out_part(c, 0)
    for h in range(1, HEADS):
        acc += out_part(c, h)
    for h in range(HEADS):
        arrived(mx.at[oc, h], mx_r.at[h], mx_s.at[h])
        acc += out_part(oc, h)
    out_ref[...] = acc.astype(BF)

    for cp in sends:
        cp.wait_send()
    for k in range(TAILS):
        pl.when(g < NG - 1)(tails[k].wait_send)
        if k:
            pl.when(row_start)(relayed[k].wait_send)
    for cp in across:
        pl.when(follows)(cp.wait_send)


def shards(tokens, w_query, w_key, w_value, w_out, slot_query, span_decay, ffn_up, ffn_down, norm_gain):
    V = pltpu.VMEM
    DMA = pltpu.SemaphoreType.DMA
    scratch = [
        V((2, HALF, D), BF), V((2, HALF, D), BF),
        V((D, HC), BF), V((D, HC), BF), V((D, HC), BF), V((D, HC), BF),
        V((MEM, HC), BF), V((1, HEADS), F32), V((1, D), F32),
        V((2, HALF, HC), BF), V((2, HALF, HC), BF), V((2, HALF, HC), BF),
        V((2, HALF, HC), BF), V((2, HALF, HC), BF),
        V((NZ, NY, 2, NX, 8, FS), BF),
        V((NX, ROWS, HS), BF), V((2, 8, 128), F32), V((2, 128, 128), F32),
        V((NX, ROWS, HS), BF), V((NX, 8, 128), F32),
        V((NY, ROWS, HS), BF), V((NY, 8, 128), F32),
        V((NZ, ROWS, HS), BF), V((NZ, 8, 128), F32),
        V((2, NX, NX * PART, HC), BF),
        V((NX, 2 * PART, D), BF), V((NX - 1, 2 * PART, D), BF), V((2 * MEM, D), F32),
        V((2, 2 * MEM, HC), BF), V((2, 2 * MEM, HC), BF), V((2, 2 * MEM, FS), BF),
        V((2, 2 * PART, D), BF),
        V((2, HALF, HC), F32),
        V((MEM, HC), BF), V((MEM, HC), BF),
        V((2, HEADS, 2 * HALF, HS), BF),
        V((128, 128), F32), V((TAILS, HALF // TAILS, D), BF),
        DMA((8,)), DMA((2,)), DMA((3,)), DMA((3,)), DMA((TAILS,)), DMA((TAILS,)), DMA((TAILS,)), DMA((TAILS,)),
        DMA((2, NX - 1)), DMA((2, NX - 1)), DMA((2, 2, NZ // 2)), DMA((2, 2, NZ // 2)),
        DMA((2, NZ)), DMA((2, NZ)), DMA, DMA,
        DMA((2, NX - 1)), DMA((2, NX - 1)), DMA((2, NY - 1)), DMA((2, NY - 1)),
        DMA((2, NZ - 1)), DMA((2, NZ - 1)),
        DMA((2, NX)), DMA((2, NX)), DMA((2,)), DMA((2,)), DMA((NX,)), DMA((NX,)), DMA, DMA, DMA((HEADS,)), DMA((HEADS,)),
    ]
    args = (
        tokens, w_query, w_key, w_value, w_out, slot_query, span_decay, ffn_up,
        ffn_down.T, norm_gain.reshape(1, D),
    )
    hbm = pl.BlockSpec(memory_space=pltpu.HBM)
    vm = pl.BlockSpec(memory_space=pltpu.VMEM)
    return pl.pallas_call(
        body,
        out_shape=jax.ShapeDtypeStruct((2 * HALF, HC), BF),
        in_specs=[hbm] * 10,
        out_specs=vm,
        scratch_shapes=scratch,
        compiler_params=pltpu.CompilerParams(
            collective_id=0, has_side_effects=True, vmem_limit_bytes=48 * 1024 * 1024
        ),
    )(*[pltpu.with_memory_space_constraint(a, pltpu.HBM) for a in args])


def solution(mesh):
    in_specs = (
        P(("group", "seq"), None),
        P(None, "seq"),
        P(None, "seq"),
        P(None, "seq"),
        P(None, "seq"),
        P(None, "seq"),
        P("group", "seq"),
        P("group", "seq"),
        P("seq", "group"),
        P(),
    )
    out_specs = P("group", "seq")
    return jax.shard_map(shards, mesh=mesh, in_specs=in_specs, out_specs=out_specs, check_vma=False)
```

```python
import jax
import jax.numpy as jnp
from jax import lax
from jax.experimental import pallas as pl
from jax.experimental.pallas import tpu as pltpu
from jax.sharding import PartitionSpec as P

HS = 128
MEM = 64
NX, NY, NZ = 4, 4, 8
NG = NX * NY * NZ
HALF = 256
HC = 512
HEADS = 4
D = 1024
PART = MEM // NX
ROWS = HEADS * PART
FS = 512
TAILS = 4
FORWARD = (1, 3, 2)
MESH = pl.DeviceIdType.MESH
F32 = jnp.float32
BF = jnp.bfloat16
FLOOR = -1e30
NULL = 8.0
SCALE = HS ** (-0.5)
LOG2E = 1.4426950408889634


def nn(a, b):
    return lax.dot_general(a, b, (((1,), (0,)), ((), ())), preferred_element_type=F32)


def nt(a, b):
    return lax.dot_general(a, b, (((1,), (1,)), ((), ())), preferred_element_type=F32)


def stat_columns(peak, mass, rate, rows):
    lane = lax.broadcasted_iota(jnp.int32, (rows, 128), 1)
    return jnp.where(lane == 0, peak, jnp.where(lane == 1, mass, jnp.where(lane == 2, rate, 0.0)))


def before_item(items, stop):
    rate = jnp.zeros_like(items[0][0])
    shifted = [None] * len(items)
    for k in reversed(range(len(items))):
        live = k < stop
        shifted[k] = jnp.where(live, items[k][0] - rate, FLOOR)
        rate = rate + jnp.where(live, items[k][2], 0.0)
    peak = shifted[0]
    for a in shifted[1:]:
        peak = jnp.maximum(peak, a)
    weights = [jnp.where(k < stop, jnp.exp(a - peak), 0.0) for k, a in enumerate(shifted)]
    mass = jnp.zeros_like(rate)
    for w, item in zip(weights, items):
        mass = mass + item[1] * w
    return (peak, mass, rate), weights


def weighted(cols, first, values):
    total = cols[:, first : first + 1] * values[0].astype(F32)
    for k in range(1, len(values)):
        total = total + cols[:, first + k : first + k + 1] * values[k].astype(F32)
    return total


def body(
    tok_h, wq_h, wk_h, wv_h, wo_h, slot_h, decay_h, up_h, dn_h, gain_h, out_ref,
    tok, ptok, wq, wk, wv, wo, slot_ref, decay_ref, gain_ref, qs, ks, vs, kp, vp, ff,
    ps, pst, sc, xr, xst, yr, yst, zr, zst, fm, pb, rs, own, pc, pc_in, hid, st, lo, mk, mv, mx,
    tr, relay, load_sem, loc_sem, tok_s, tok_r, tail_s, tail_r, relay_s, relay_r, wx_s, wx_r, rg_s, rg_r, ny_s, ny_r, fy_s, fy_r,
    x_s, x_r, y_s, y_r, z_s, z_r, fm_s, fm_r, pc_s, pc_r, rs_s, rs_r, st_s, st_r, mx_s, mx_r,
):
    g = lax.axis_index("group")
    c = lax.axis_index("seq")
    x = lax.rem(g, NX)
    y = lax.rem(g // NX, NY)
    z = g // (NX * NY)
    oc = 1 - c

    def gid(zz, yy, xx):
        return zz * (NX * NY) + yy * NX + xx

    def xp(d):
        return lax.rem(x + d, NX)

    def yp(d):
        return lax.rem(y + d, NY)

    def zp(d):
        return lax.rem(z + d, NZ)

    nxt = lax.rem(g + 1, NG)
    prv = lax.rem(g + NG - 1, NG)
    down_row, up_row = lax.rem(g + NX, NG), lax.rem(g + NG - NX, NG)
    sends = []

    def send(src, dst, ss, rsem, gg, cc):
        cp = pltpu.make_async_remote_copy(
            src_ref=src, dst_ref=dst, send_sem=ss, recv_sem=rsem,
            device_id={"group": gg, "seq": cc}, device_id_type=MESH,
        )
        cp.start()
        sends.append(cp)
        return cp

    def arrived(ref, sem, ss):
        pltpu.make_async_remote_copy(
            src_ref=ref, dst_ref=ref, send_sem=ss, recv_sem=sem,
            device_id={"group": g, "seq": oc}, device_id_type=MESH,
        ).wait_recv()

    tr[...] = jnp.zeros_like(tr)
    barrier = pltpu.get_barrier_semaphore()

    def greet(gg, cc):
        pl.semaphore_signal(barrier, inc=1, device_id={"group": gg, "seq": cc}, device_id_type=MESH)

    greet(g, oc)
    for d in range(1, NX):
        greet(gid(z, y, xp(d)), c)
        greet(gid(z, y, xp(d)), oc)
    for d in range(1, NY):
        greet(gid(z, yp(d), x), c)
    for d in range(1, NZ):
        greet(gid(zp(d), y, x), c)
    greet(nxt, c)
    greet(prv, c)
    greet(down_row, c)
    greet(up_row, c)

    loads = []
    for k, (src, dst) in enumerate(
        (
            (tok_h, tok.at[c]), (wk_h, wk), (wv_h, wv), (wq_h, wq), (wo_h, wo),
            (slot_h, slot_ref), (decay_h, decay_ref), (gain_h, gain_ref),
        )
    ):
        cp = pltpu.make_async_copy(src, dst, load_sem.at[k])
        cp.start()
        loads.append(cp)
    lanes_x = pl.ds(pl.multiple_of(x * FS, FS), FS)
    wl = []
    for k, (src, dst) in enumerate(((up_h, ff), (dn_h, ff))):
        cp = pltpu.make_async_copy(src.at[:, lanes_x], dst.at[z, y, k, x], loc_sem.at[k])
        cp.start()
        wl.append(cp)

    def project(half):
        rows = tok[half]
        ks[half] = nn(rows, wk[...]).astype(BF)
        vs[half] = nn(rows, wv[...]).astype(BF)

    pl.semaphore_wait(barrier, 2 * (NX - 1) + (NY - 1) + (NZ - 1) + 5)

    pieces = ((slice(0, HALF // 2), 0), (slice(HALF // 2, HALF), 3))
    for r, k in pieces:
        send(tok_h.at[r], tok.at[c, r], tok_s.at[k], tok_r.at[k], g, oc)
    for k, (src, dst) in enumerate(((up_h, ff), (dn_h, ff))):
        for d in range(1, NX):
            to = xp(d)
            send(
                src.at[:, pl.ds(pl.multiple_of(to * FS, FS), FS)], dst.at[z, y, k, x],
                wx_s.at[k, d - 1], wx_r.at[k, d - 1], gid(z, y, to), c,
            )

    row_end = (x == NX - 1) & (g < NG - 1)
    row_start = (x == 0) & (g < NG - NX)
    follows = g > 0
    tails, handed, relayed = [], [], []
    for k in range(TAILS):
        rows = slice(k * (HALF // TAILS), (k + 1) * (HALF // TAILS))

        def piece(src, dst, ss, rsem, to):
            return pltpu.make_async_remote_copy(
                src_ref=src, dst_ref=dst, send_sem=ss, recv_sem=rsem,
                device_id={"group": to, "seq": c}, device_id_type=MESH,
            )

        there = ptok.at[c, rows]
        tails.append(piece(tok_h.at[rows], there, tail_s.at[k], tail_r.at[k], nxt))
        handed.append(
            piece(tok_h.at[rows], relay.at[k], tail_s.at[k], relay_r.at[k], gid(z, y, 0))
        )
        relayed.append(piece(relay.at[k], there, relay_s.at[k], tail_r.at[k], down_row))

    def tail_start(k, cond):
        pl.when(cond)(tails[k].start)

    def relay_start(k, cond):
        @pl.when(row_start & cond)
        def _():
            handed[k].wait_recv()
            relayed[k].start()

    tail_start(0, row_end)
    for cp in loads[:3]:
        cp.wait()
    project(c)

    left_y, right_y = yp(NY - 1), yp(1)
    left_z, right_z = zp(NZ - 1), zp(1)

    def weights_x():
        for k in range(2):
            wl[k].wait()
            for d in range(1, NX):
                arrived(ff.at[z, y, k, xp(NX - d)], wx_r.at[k, d - 1], wx_s.at[k, d - 1])

    def weights_ring(step, row=y, lane=0):
        a, b = ff.at[zp(NZ + 1 - step), row], ff.at[zp(step - 1), row]
        if step == NZ // 2:
            a, b = a.at[0], b.at[1]
        k = step - 1
        send(a, a, rg_s.at[lane, 0, k], rg_r.at[lane, 0, k], gid(right_z, y, x), c)
        send(b, b, rg_s.at[lane, 1, k], rg_r.at[lane, 1, k], gid(left_z, y, x), c)

    def ring_wait(step, row=y, lane=0):
        a, b = ff.at[zp(NZ - step), row], ff.at[zp(step), row]
        if step == NZ // 2:
            a, b = a.at[0], b.at[1]
        arrived(a, rg_r.at[lane, 0, step - 1], rg_s.at[lane, 0, step - 1])
        arrived(b, rg_r.at[lane, 1, step - 1], rg_s.at[lane, 1, step - 1])

    far_y = yp(2)

    def far_ring(step):
        if step == 1:
            arrived(ff.at[z, far_y], fy_r, fy_s)
        else:
            ring_wait(step - 1, far_y, 1)
        weights_ring(step, far_y, 1)

    def weights_near(o):
        b = ff.at[zp(o), y]
        send(b, b, ny_s.at[0, o], ny_r.at[0, o], gid(z, right_y, x), c)
        send(b, b, ny_s.at[1, o], ny_r.at[1, o], gid(z, left_y, x), c)

    def near_wait(o):
        arrived(ff.at[zp(o), left_y], ny_r.at[0, o], ny_s.at[0, o])
        arrived(ff.at[zp(o), right_y], ny_r.at[1, o], ny_s.at[1, o])

    def weights_far():
        near_wait(0)
        b = ff.at[z, left_y]
        send(b, b, fy_s, fy_r, gid(z, right_y, x), c)

    def weights_done():
        for o in range(1, NZ):
            near_wait(o)
        ring_wait(NZ // 2, far_y, 1)

    for r, k in pieces:
        arrived(tok.at[oc, r], tok_r.at[k], tok_s.at[k])
        rows = tok[oc, r]
        ks[oc, r] = nn(rows, wk[...]).astype(BF)
        vs[oc, r] = nn(rows, wv[...]).astype(BF)

    loads[5].wait()
    loads[6].wait()
    for h in range(HEADS):
        cols = slice(h * HS, (h + 1) * HS)
        keys = ks[:, :, cols].reshape(2 * HALF, HS)
        vals = vs[:, :, cols].reshape(2 * HALF, HS)
        scores = nt(slot_ref[:, cols], keys) * SCALE
        peak = jnp.max(scores, axis=1, keepdims=True)
        w = jnp.exp(scores - peak)
        mass = jnp.sum(w, axis=1, keepdims=True)
        pooled = nn(w.astype(BF), vals)
        stat = stat_columns(peak, mass, decay_ref[0:1, h : h + 1], MEM)
        for p in range(NX):
            rows = slice(p * PART, (p + 1) * PART)
            ps[p, h * PART : (h + 1) * PART, :] = pooled[rows].astype(BF)
            first = (p % 2) * ROWS + h * PART
            sc[p // 2, first : first + PART, :] = stat[rows]
    for q in range(2):
        pst[q] = jnp.transpose(sc[q])[0:8]

    for d in range(1, NX):
        to = xp(d)
        send(ps.at[to], xr.at[x], x_s.at[0, d - 1], x_r.at[0, d - 1], gid(z, y, to), c)
        send(pst.at[to // 2], xst.at[x], x_s.at[1, d - 1], x_r.at[1, d - 1], gid(z, y, to), c)
    for k in range(TAILS):
        tail_start(k, x < NX - 1)
        if k:
            pl.when(row_end)(handed[k].start)
    xr[x] = ps[x]
    xst[x] = pst[x // 2]
    weights_x()
    weights_ring(1)
    weights_near(0)
    loads[3].wait()
    for half in range(2):
        qs[half] = nn(tok[half], wq[...]).astype(BF)
    for d in range(1, NX):
        frm = xp(NX - d)
        arrived(xr.at[frm], x_r.at[0, d - 1], x_s.at[0, d - 1])
        arrived(xst.at[frm], x_r.at[1, d - 1], x_s.at[1, d - 1])
    odd = lax.rem(x, 2) == 1
    items = []
    for k in range(NX):
        tile = xst[k]
        tile = jnp.where(odd, pltpu.roll(tile, 64, 1), tile)
        items.append(tuple(tile[r : r + 1] for r in range(3)))
    in_row = [before_item(items, j) for j in range(NX + 1)]
    n = 0
    for j in range(1, NX + 1):
        for k in range(j):
            tr[n : n + 1] = in_row[j][1][k]
            n += 1
    cols = jnp.transpose(tr[...])[0:ROWS]
    row_val = [None]
    n = 0
    for j in range(1, NX + 1):
        row_val.append(weighted(cols, n, [xr[k] for k in range(j)]))
        n += j

    def stat_tile(state):
        sub = lax.broadcasted_iota(jnp.int32, (8, 128), 0)
        return jnp.where(sub == 0, state[0], jnp.where(sub == 1, state[1], state[2]))

    yr[y] = row_val[NX].astype(BF)
    yst[y] = stat_tile(in_row[NX][0])
    for d in range(1, NY):
        to = gid(z, yp(d), x)
        send(yr.at[y], yr.at[y], y_s.at[0, d - 1], y_r.at[0, d - 1], to, c)
        send(yst.at[y], yst.at[y], y_s.at[1, d - 1], y_r.at[1, d - 1], to, c)
    ring_wait(1)
    weights_ring(2)
    weights_far()
    weights_near(1)
    weights_near(NZ - 1)
    for d in range(1, NY):
        frm = yp(NY - d)
        arrived(yr.at[frm], y_r.at[0, d - 1], y_s.at[0, d - 1])
        arrived(yst.at[frm], y_r.at[1, d - 1], y_s.at[1, d - 1])
    items = [tuple(yst[k, r : r + 1] for r in range(3)) for k in range(NY)]
    in_plane, w_some = before_item(items, y)
    plane, w_all = before_item(items, NY)
    for k in range(NY):
        tr[k : k + 1] = w_all[k]
        tr[NY + k : NY + k + 1] = w_some[k]
    cols = jnp.transpose(tr[...])[0:ROWS]
    vals = [yr[k] for k in range(NY)]

    zr[z] = weighted(cols, 0, vals).astype(BF)
    zst[z] = stat_tile(plane)
    for d in range(1, NZ):
        to = gid(zp(d), y, x)
        send(zr.at[z], zr.at[z], z_s.at[0, d - 1], z_r.at[0, d - 1], to, c)
        send(zst.at[z], zst.at[z], z_s.at[1, d - 1], z_r.at[1, d - 1], to, c)
    plane_val = weighted(cols, NY, vals)
    far_ring(1)
    ring_wait(2)
    weights_ring(3)
    weights_near(2)
    weights_near(NZ - 2)
    relay_start(1, y < NY - 1)
    for d in range(1, NZ):
        frm = zp(NZ - d)
        arrived(zr.at[frm], z_r.at[0, d - 1], z_s.at[0, d - 1])
        arrived(zst.at[frm], z_r.at[1, d - 1], z_s.at[1, d - 1])
    items = [tuple(zst[k, r : r + 1] for r in range(3)) for k in range(NZ)]
    planes, w_some = before_item(items, z)
    for k in range(NZ):
        tr[k : k + 1] = w_some[k]
    n = NZ
    for j in range(NX):
        own_peak, own_mass, own_rate = in_row[j][0]
        shifted = [planes[0] - in_plane[2] - own_rate, in_plane[0] - own_rate, own_peak]
        peak = jnp.maximum(jnp.maximum(shifted[0], shifted[1]), shifted[2])
        parts = [jnp.exp(a - peak) for a in shifted]
        mass = planes[1] * parts[0] + in_plane[1] * parts[1] + own_mass * parts[2]
        anchor = jnp.maximum(peak, NULL)
        factor = jnp.exp(peak - anchor)
        coef = factor / (mass * factor + jnp.exp(NULL - anchor))
        for part in parts:
            tr[n : n + 1] = part * coef
            n += 1
    cols = jnp.transpose(tr[...])[0:ROWS]
    planes_val = weighted(cols, 0, [zr[k] for k in range(NZ)])
    for j in range(NX):
        vals = [planes_val, plane_val] + ([row_val[j]] if j else [])
        memory = weighted(cols, NZ + 3 * j, vals).astype(BF)
        for h in range(HEADS):
            fm[c, x, j * PART : (j + 1) * PART, h * HS : (h + 1) * HS] = memory[
                h * PART : (h + 1) * PART
            ]
    b = fm.at[c, x]
    for d in range(1, NX):
        send(b, b, fm_s.at[0, d], fm_r.at[0, d], gid(z, y, xp(d)), c)
    send(b, b, fm_s.at[1, 0], fm_r.at[1, 0], g, oc)
    far_ring(2)
    ring_wait(3)
    weights_ring(4)
    weights_near(3)
    weights_near(NZ - 3)
    relay_start(1, y == NY - 1)
    ring_wait(NZ // 2)
    weights_near(NZ // 2)
    far_ring(3)
    quarter = HALF // 2
    parts = [slice(j * quarter, (j + 1) * quarter) for j in range(2)]
    across = [
        pltpu.make_async_remote_copy(
            src_ref=ptok.at[c, r], dst_ref=ptok.at[c, r], send_sem=tok_s.at[1 + j],
            recv_sem=tok_r.at[1 + j], device_id={"group": g, "seq": oc}, device_id_type=MESH,
        )
        for j, r in enumerate(parts)
    ]

    def project_prev(half, r):
        rows = ptok[half, r]
        kp[half, r] = nn(rows, wk[...]).astype(BF)
        vp[half, r] = nn(rows, wv[...]).astype(BF)

    def prev_take(j):
        for k in range(j * TAILS // 2, (j + 1) * TAILS // 2):
            tails[k].wait_recv()
        across[j].start()
        project_prev(c, parts[j])

    def prev_rest(j):
        arrived(ptok.at[oc, parts[j]], tok_r.at[1 + j], tok_s.at[1 + j])
        project_prev(oc, parts[j])

    for d in FORWARD:
        b = fm.at[c, xp(NX - d)]
        arrived(b, fm_r.at[0, d], fm_s.at[0, d])
        send(b, b, fm_s.at[1, d], fm_r.at[1, d], g, oc)
    pl.when(follows)(lambda: prev_take(0))
    far_ring(NZ // 2)
    relay_start(2, True)
    relay_start(3, True)
    pl.when(follows)(lambda: prev_rest(0))
    arrived(fm.at[oc, x], fm_r.at[1, 0], fm_s.at[1, 0])
    for d in FORWARD:
        arrived(fm.at[oc, xp(NX - d)], fm_r.at[1, d], fm_s.at[1, d])
    weights_done()
    up = ff[:, :, 0].reshape(D, FS)
    total = nn(fm[0].reshape(NX * MEM, HC), up[0:HC]) + nn(fm[1].reshape(NX * MEM, HC), up[HC:])
    hid[...] = jax.nn.gelu(total, approximate=True).astype(BF).reshape(2, 2 * MEM, FS)
    down = ff[:, :, 1].reshape(D, FS)
    for k in range(2):
        pc[k] = nt(hid[oc], down[k * HC : (k + 1) * HC]).astype(BF)
        send(pc.at[k], pc_in.at[k], pc_s.at[k], pc_r.at[k], g, oc)
    own[...] = nt(hid[c], down)
    for k in range(2):
        arrived(pc_in.at[k], pc_r.at[k], pc_s.at[k])
    own[...] += jnp.concatenate([pc_in[0], pc_in[1]], 1).astype(F32)
    for j in range(NX):
        for q in range(2):
            first = q * MEM + j * PART
            pb[j, q * PART : (q + 1) * PART, :] = own[first : first + PART].astype(BF)
    for d in FORWARD:
        to = xp(d)
        send(pb.at[to], rs.at[d - 1], rs_s.at[d], rs_r.at[d], gid(z, y, to), c)
    @pl.when(follows)
    def _():
        prev_take(1)
        prev_rest(1)

    @pl.when(g == 0)
    def _():
        kp[...] = jnp.zeros_like(kp)
        vp[...] = jnp.zeros_like(vp)

    row_i = lax.broadcasted_iota(jnp.int32, (HALF, HALF), 0)
    col_i = lax.broadcasted_iota(jnp.int32, (HALF, HALF), 1)
    tri = col_i <= row_i
    bias = jnp.where(g == 0, FLOOR, 0.0).astype(F32)

    def attend(h, i):
        cols = slice(h * HS, (h + 1) * HS)
        q = qs[i, :, cols]
        near = nt(q, ks[i, :, cols])
        far = nt(q, kp[i, :, cols]) + bias
        diag = jnp.where(tri, near, far)
        if i == 0:
            full = nt(q, kp[1, :, cols]) + bias
            full_v = vp[1, :, cols]
        else:
            full = nt(q, ks[0, :, cols])
            full_v = vs[0, :, cols]
        high = jnp.maximum(
            jnp.max(diag, axis=1, keepdims=True), jnp.max(full, axis=1, keepdims=True)
        )
        ed = jnp.exp2((diag - high) * (SCALE * LOG2E))
        ef = jnp.exp2((full - high) * (SCALE * LOG2E))
        mass = jnp.sum(ed, axis=1, keepdims=True) + jnp.sum(ef, axis=1, keepdims=True)
        acc = nn(jnp.where(tri, ed, 0.0).astype(BF), vs[i, :, cols])
        acc += nn(jnp.where(tri, 0.0, ed).astype(BF), vp[i, :, cols])
        acc += nn(ef.astype(BF), full_v)
        lo[i, :, cols] = acc / mass

    for h in range(HEADS):
        for i in range(2):
            attend(h, i)
    loads[4].wait()
    loads[7].wait()
    for d in FORWARD:
        arrived(rs.at[d - 1], rs_r.at[d], rs_s.at[d])
    mine = pl.ds(pl.multiple_of(x * PART, PART), PART)
    acc = jnp.concatenate(
        [own[pl.ds(pl.multiple_of(q * MEM + x * PART, PART), PART), :] for q in range(2)], 0
    )
    mem = fm[:, pl.ds(2 * c, 2), mine, :]
    mem = jnp.concatenate(
        [mem[0].reshape(2 * PART, HC), mem[1].reshape(2 * PART, HC)], 1
    ).astype(F32)
    for d in range(NX - 1):
        acc += rs[d].astype(F32)
    summed = mem + acc
    scaled = summed * lax.rsqrt(jnp.mean(summed * summed, axis=-1, keepdims=True) + 1e-06)
    st[c] = (scaled * gain_ref[...]).astype(BF)
    send(st.at[c], st.at[c], st_s, st_r, g, oc)
    arrived(st.at[oc], st_r, st_s)
    settled = st[...].reshape(MEM, D)
    mk[...] = nn(settled, wk[...]).astype(BF)
    mv[...] = nn(settled, wv[...]).astype(BF)

    def out_part(cc, h):
        return nn(mx[cc, h], wo[pl.ds(pl.multiple_of(cc * HC + h * HS, HS), HS), :])

    def cross_head(h):
        cols = slice(h * HS, (h + 1) * HS)
        q = qs[:, :, cols].reshape(2 * HALF, HS)
        scores = nt(q, mk[:, cols])
        high = jnp.max(scores, axis=1, keepdims=True)
        e = jnp.exp2((scores - high) * (SCALE * LOG2E))
        probs = (e / jnp.sum(e, axis=1, keepdims=True)).astype(BF)
        both = lo[:, :, cols].reshape(2 * HALF, HS) + nn(probs, mv[:, cols])
        return both.astype(BF)

    for h in range(0, HEADS, 2):
        pair = [cross_head(h), cross_head(h + 1)]
        for k in range(2):
            mx[c, h + k] = pair[k]
        for k in range(2):
            b = mx.at[c, h + k]
            send(b, b, mx_s.at[h + k], mx_r.at[h + k], g, oc)
    acc = out_part(c, 0)
    for h in range(1, HEADS):
        acc += out_part(c, h)
    for h in range(HEADS):
        arrived(mx.at[oc, h], mx_r.at[h], mx_s.at[h])
        acc += out_part(oc, h)
    out_ref[...] = acc.astype(BF)

    for cp in sends:
        cp.wait_send()
    for k in range(TAILS):
        pl.when(g < NG - 1)(tails[k].wait_send)
        if k:
            pl.when(row_start)(relayed[k].wait_send)
    for cp in across:
        pl.when(follows)(cp.wait_send)


def shards(tokens, w_query, w_key, w_value, w_out, slot_query, span_decay, ffn_up, ffn_down, norm_gain):
    V = pltpu.VMEM
    DMA = pltpu.SemaphoreType.DMA
    scratch = [
        V((2, HALF, D), BF), V((2, HALF, D), BF),
        V((D, HC), BF), V((D, HC), BF), V((D, HC), BF), V((D, HC), BF),
        V((MEM, HC), BF), V((1, HEADS), F32), V((1, D), F32),
        V((2, HALF, HC), BF), V((2, HALF, HC), BF), V((2, HALF, HC), BF),
        V((2, HALF, HC), BF), V((2, HALF, HC), BF),
        V((NZ, NY, 2, NX, 8, FS), BF),
        V((NX, ROWS, HS), BF), V((2, 8, 128), F32), V((2, 128, 128), F32),
        V((NX, ROWS, HS), BF), V((NX, 8, 128), F32),
        V((NY, ROWS, HS), BF), V((NY, 8, 128), F32),
        V((NZ, ROWS, HS), BF), V((NZ, 8, 128), F32),
        V((2, NX, NX * PART, HC), BF),
        V((NX, 2 * PART, D), BF), V((NX - 1, 2 * PART, D), BF), V((2 * MEM, D), F32),
        V((2, 2 * MEM, HC), BF), V((2, 2 * MEM, HC), BF), V((2, 2 * MEM, FS), BF),
        V((2, 2 * PART, D), BF),
        V((2, HALF, HC), F32),
        V((MEM, HC), BF), V((MEM, HC), BF),
        V((2, HEADS, 2 * HALF, HS), BF),
        V((128, 128), F32), V((TAILS, HALF // TAILS, D), BF),
        DMA((8,)), DMA((2,)), DMA((4,)), DMA((4,)), DMA((TAILS,)), DMA((TAILS,)), DMA((TAILS,)), DMA((TAILS,)),
        DMA((2, NX - 1)), DMA((2, NX - 1)), DMA((2, 2, NZ // 2)), DMA((2, 2, NZ // 2)),
        DMA((2, NZ)), DMA((2, NZ)), DMA, DMA,
        DMA((2, NX - 1)), DMA((2, NX - 1)), DMA((2, NY - 1)), DMA((2, NY - 1)),
        DMA((2, NZ - 1)), DMA((2, NZ - 1)),
        DMA((2, NX)), DMA((2, NX)), DMA((2,)), DMA((2,)), DMA((NX,)), DMA((NX,)), DMA, DMA, DMA((HEADS,)), DMA((HEADS,)),
    ]
    args = (
        tokens, w_query, w_key, w_value, w_out, slot_query, span_decay, ffn_up,
        ffn_down.T, norm_gain.reshape(1, D),
    )
    hbm = pl.BlockSpec(memory_space=pltpu.HBM)
    vm = pl.BlockSpec(memory_space=pltpu.VMEM)
    return pl.pallas_call(
        body,
        out_shape=jax.ShapeDtypeStruct((2 * HALF, HC), BF),
        in_specs=[hbm] * 10,
        out_specs=vm,
        scratch_shapes=scratch,
        compiler_params=pltpu.CompilerParams(
            collective_id=0, has_side_effects=True, vmem_limit_bytes=48 * 1024 * 1024
        ),
    )(*[pltpu.with_memory_space_constraint(a, pltpu.HBM) for a in args])


def solution(mesh):
    in_specs = (
        P(("group", "seq"), None),
        P(None, "seq"),
        P(None, "seq"),
        P(None, "seq"),
        P(None, "seq"),
        P(None, "seq"),
        P("group", "seq"),
        P("group", "seq"),
        P("seq", "group"),
        P(),
    )
    out_specs = P("group", "seq")
    return jax.shard_map(shards, mesh=mesh, in_specs=in_specs, out_specs=out_specs, check_vma=False)
```
